256 devices in a mesh: dp: 8 (over z), fsdp: 16 (over x, y), tensor: 2 (over core).
Axes of the slice: x: 4, y: 4, z: 8, core: 2. Of those that a mesh axis runs over, the one named last changes fastest.
Arguments:
- tokens: bfloat16 [32768, 2048], P('fsdp'), may hold values from -6 to 6
- segment_ids: int32 [32768], P('fsdp'), may hold values from 0 to 127, never falling along the last dimension, each value on 1 to 512 neighbouring positions
- row_order: int32 [32768], P('fsdp'), may hold values from 0 to 2047, as said below
- row_counts: int32 [16], replicated, may hold values from 0 to 1280, as said below
- first_gain: float32 [2048], replicated, may hold values from 0.25 to 1.75
- second_gain: float32 [2048], replicated, may hold values from 0.25 to 1.75
- query_weight: bfloat16 [2048, 2048], P('fsdp', ('dp', 'tensor')), may hold values from -0.110485435 to 0.110485435
- key_weight: bfloat16 [2048, 2048], P('fsdp', ('dp', 'tensor')), may hold values from -4.4636116 to 4.4636116
- value_weight: bfloat16 [2048, 2048], P('fsdp', ('dp', 'tensor')), may hold values from -0.125 to 0.125
- output_weight: bfloat16 [2048, 2048], P(('dp', 'tensor'), 'fsdp'), may hold values from -0.125 to 0.125
- gate_weight: bfloat16 [2048, 8192], P('fsdp', ('dp', 'tensor')), may hold values from -0.125 to 0.125
- up_weight: bfloat16 [2048, 8192], P('fsdp', ('dp', 'tensor')), may hold values from -0.125 to 0.125
- down_weight: bfloat16 [8192, 2048], P(('dp', 'tensor'), 'fsdp'), may hold values from -0.0625 to 0.0625
Outputs:
- recursed: bfloat16 [32768, 2048], P('fsdp', ('dp', 'tensor'))
The draws below stay inside these ranges and needn't reach their ends.
Inputs may be any that keep to these rules, and one draw needn't show every extreme that they name: `row_counts`: each entry is a multiple of 128, the entries sum to 16384, and the largest entry is exactly 1280. `row_order`: each shard's block of 2048 entries is a permutation of 0 to 2047.
All inputs are finite; a program needn't handle non-finite values.
Results may differ from the reference program's by a relative error of at most 0.015.
Values may be sent and summed in bfloat16 or wider, within the bound.
A program may use at most 128 MiB of HBM per device.

```python
import math
import jax
import jax.numpy as jnp
import numpy as np
from jax import lax

D = 2048
HEAD = 128
FF_DEV = 512
TOK_DEV = 2048
TILE = 128
HEADS = 16
INNER = 2048
FF = 8192
SHARDS = 16
TOKENS = 32768
TILES = 16
CAP_TILES = 10
N_DP = 8
N_TENSOR = 2


def draw_row_counts(key, part):
    quota = TILES // 2
    slot_total = SHARDS * CAP_TILES
    owners = jnp.arange(slot_total, dtype=jnp.int32) // CAP_TILES
    full_shard = jax.random.randint(jax.random.fold_in(key, 11), (), 0, SHARDS).astype(jnp.int32)
    shuffled = jax.random.permutation(jax.random.fold_in(key, 12), slot_total).astype(jnp.int32)
    ranks = jnp.zeros((slot_total,), jnp.int32).at[shuffled].set(jnp.arange(slot_total, dtype=jnp.int32))
    ranks = jnp.where(owners == full_shard, -1, ranks)
    ordered = jnp.argsort(ranks, stable=True).astype(jnp.int32)
    chosen = ordered[:SHARDS * quota]
    tile_counts = jnp.zeros((SHARDS,), jnp.int32).at[jnp.take(owners, chosen)].add(1)
    return (tile_counts * TILE).astype(jnp.int32)


def draw_row_order(key, part):
    shard_keys = jax.random.split(jax.random.fold_in(key, 21), SHARDS)
    orders = jax.vmap(lambda shard_key: jax.random.permutation(shard_key, TOK_DEV))(shard_keys)
    return orders.reshape(-1).astype(jnp.int32)


def query_key_pair(key):
    base_draw = jnp.clip(jax.random.normal(jax.random.fold_in(key, 31), (D, INNER), jnp.float32), -5.0, 5.0) / math.sqrt(D)
    other_draw = jnp.clip(jax.random.normal(jax.random.fold_in(key, 32), (D, INNER), jnp.float32), -5.0, 5.0) / math.sqrt(D)
    return (base_draw, other_draw)


def draw_query_weight(key, part):
    return query_key_pair(key)[0].astype(jnp.bfloat16)


def draw_key_weight(key, part):
    return query_key_pair(key)[1].astype(jnp.bfloat16)


def levels(key, extent, pieces, smallest, top_value):
    def one(position, shards_of):
        heights = jax.random.uniform(jax.random.fold_in(jax.random.fold_in(key, 6), position), (shards_of,), jnp.float32, smallest / len(pieces), top_value / len(pieces))
        return jnp.repeat(jnp.exp(heights), extent[position] // shards_of).reshape((-1,) + (1,) * (len(extent) - position - 1))

    loudness = one(*pieces[0])
    for cut in pieces[1:]:
        loudness = loudness * one(*cut)
    return loudness


def split_up(number_of, total, limit, lean):
    portions = [(1 << 20) // math.isqrt(rank ** lean) + 1 for rank in range(2, number_of + 1)]
    surplus, counts = total - limit - (number_of - 1), [1] * (number_of - 1)
    while surplus > 0:
        free = [i for i in range(number_of - 1) if counts[i] < limit]
        whole, budget = sum([portions[i] for i in free]), surplus
        for i in free:
            more = min(limit - counts[i], max(1, budget * portions[i] // whole), surplus)
            counts[i] = counts[i] + more
            surplus = surplus - more
    return np.array([limit] + counts)


def uneven_parts(key, number_of, total, bound, slope):
    if number_of == 2:
        one = jax.random.randint(key, (), max(1, total - bound), min(bound, total - 1) + 1)
        return jnp.stack([one, total - one])
    lengths = jnp.asarray(split_up(number_of, total, bound, slope), jnp.int32)
    twos = (number_of - 1) // 2
    source_of, receiver = lengths[1:1 + 2 * twos:2], lengths[2:2 + 2 * twos:2]
    margin = jnp.minimum(source_of - 1, bound - receiver)
    moved = jax.random.randint(jax.random.fold_in(key, 1), (twos,), 0, 1 << 20) % (margin + 1)
    lengths = lengths.at[1:1 + 2 * twos:2].set(source_of - moved).at[2:2 + 2 * twos:2].set(receiver + moved)
    return lengths[jax.random.permutation(jax.random.fold_in(key, 2), number_of)]


def scatter_about(key, extent, width, limit, pieces=(), kind=jnp.bfloat16):
    entries = jax.random.normal(key, extent, jnp.float32) * width
    if len(pieces) > 0:
        entries = levels(key, extent, pieces, -0.22, 0.18) * entries
    return jnp.clip(entries, min=-limit, max=limit).astype(kind)


def setup_inputs(seed: int = 0) -> dict:
    splits = jax.random.split(jax.random.key(seed), 14)
    return {
        "tokens": scatter_about(splits[0], (TOKENS, D), 1.0, 6.0, ((0, 16),)),
        "segment_ids": jnp.searchsorted(jnp.cumsum(uneven_parts(splits[1], TOKENS // (2 * TILE), TOKENS, 4 * TILE, 2)), jnp.arange(TOKENS), side="right").astype(jnp.int32),
        "row_order": draw_row_order(jax.random.fold_in(splits[13], 71), 0),
        "row_counts": draw_row_counts(jax.random.fold_in(splits[13], 71), 0),
        "first_gain": jnp.clip(1.0 + 0.15 * jax.random.normal(splits[4], (D,), jnp.float32), 0.25, 1.75),
        "second_gain": jnp.clip(1.0 + 0.15 * jax.random.normal(splits[5], (D,), jnp.float32), 0.25, 1.75),
        "query_weight": draw_query_weight(jax.random.fold_in(splits[13], 71), 0),
        "key_weight": draw_key_weight(jax.random.fold_in(splits[13], 71), 0),
        "value_weight": scatter_about(splits[8], (D, INNER), D ** -0.5, 0.125, ((0, 16), (1, 16))),
        "output_weight": scatter_about(splits[9], (INNER, D), INNER ** -0.5, 0.125, ((0, 16), (1, 16))),
        "gate_weight": scatter_about(splits[10], (D, FF), D ** -0.5, 0.125, ((0, 16), (1, 16))),
        "up_weight": scatter_about(splits[11], (D, FF), D ** -0.5, 0.125, ((0, 16), (1, 16))),
        "down_weight": scatter_about(splits[12], (FF, D), FF ** -0.5, 0.0625, ((0, 16), (1, 16))),
    }


def rms_scale(row_data, gain_row):
    floats = row_data.astype(jnp.float32)
    inverse = lax.rsqrt(lax.optimization_barrier(jnp.mean(floats * floats, axis=-1, keepdims=True)) + 1e-05)
    return (floats * inverse * gain_row).astype(jnp.bfloat16)

def rounded_sum(terms):
    narrow = lax.optimization_barrier(terms.astype(jnp.bfloat16))
    return lax.optimization_barrier(jnp.sum(narrow.astype(jnp.float32), axis=1))

def reference(tokens, segment_ids, row_order, row_counts, first_gain, second_gain, query_weight, key_weight, value_weight, output_weight, gate_weight, up_weight, down_weight):
    groups = N_DP * N_TENSOR
    score_scale = 1.0 / math.sqrt(HEAD)
    positions = jnp.arange(TOK_DEV, dtype=jnp.int32)
    out_heads = output_weight.astype(jnp.float32).reshape(HEADS, HEAD, D)
    down_groups = down_weight.astype(jnp.float32).reshape(groups, FF_DEV, D)

    def one_shard(packed):
        shard_rows, shard_segs, shard_order, live_count = packed
        normed = rms_scale(shard_rows, first_gain)
        queries = jnp.dot(normed, query_weight, preferred_element_type=jnp.float32).astype(jnp.bfloat16)
        key_rows = jnp.dot(normed, key_weight, preferred_element_type=jnp.float32).astype(jnp.bfloat16)
        value_rows = jnp.dot(normed, value_weight, preferred_element_type=jnp.float32).astype(jnp.bfloat16)
        query_heads = queries.astype(jnp.float32).reshape(TOK_DEV, HEADS, HEAD)
        key_heads = key_rows.astype(jnp.float32).reshape(TOK_DEV, HEADS, HEAD)
        value_heads = value_rows.astype(jnp.float32).reshape(TOK_DEV, HEADS, HEAD)
        scores = jnp.einsum('qhd,khd->hqk', query_heads, key_heads) * score_scale
        allowed = (shard_segs[:, None] == shard_segs[None, :]) & (positions[None, :] <= positions[:, None])
        scores = jnp.where(allowed[None], scores, -1e+30)
        peak = lax.optimization_barrier(jnp.max(scores, axis=-1, keepdims=True))
        expo = jnp.exp(scores - peak)
        probs = (expo / lax.optimization_barrier(jnp.sum(expo, axis=-1, keepdims=True))).astype(jnp.bfloat16)
        attended = jnp.einsum('hqk,khd->qhd', probs.astype(jnp.float32), value_heads).astype(jnp.bfloat16)
        head_terms = jnp.einsum('qhd,hde->qhe', attended.astype(jnp.float32), out_heads)
        carried = (shard_rows.astype(jnp.float32) + rounded_sum(head_terms)).astype(jnp.bfloat16)
        normed_two = rms_scale(carried, second_gain)
        gate = jnp.dot(normed_two, gate_weight, preferred_element_type=jnp.float32)
        upward = jnp.dot(normed_two, up_weight, preferred_element_type=jnp.float32)
        hidden = (jax.nn.silu(gate) * upward).astype(jnp.bfloat16)
        hidden_groups = hidden.astype(jnp.float32).reshape(TOK_DEV, groups, FF_DEV)
        ff_terms = jnp.einsum('tgf,gfe->tge', hidden_groups, down_groups)
        updated = (carried.astype(jnp.float32) + rounded_sum(ff_terms)).astype(jnp.bfloat16)
        row_rank = jnp.zeros((TOK_DEV,), jnp.int32).at[shard_order].set(positions)
        is_live = row_rank < live_count
        return jnp.where(is_live[:, None], updated, shard_rows)
    outputs = lax.map(one_shard, (tokens.reshape(SHARDS, TOK_DEV, D), segment_ids.reshape(SHARDS, TOK_DEV), row_order.reshape(SHARDS, TOK_DEV), row_counts))
    return outputs.reshape(TOKENS, D)
```

```python
import math

import jax
import jax.numpy as jnp
from jax import lax
from jax.experimental import pallas as pl
from jax.experimental.pallas import tpu as pltpu
from jax.sharding import PartitionSpec as P

F32 = jnp.float32
BF16 = jnp.bfloat16
NZ = 8
NX = 4
NY = 4
B = 128
ROWS = 2048
D = 2048
CAP = 1280
HALF = 640
QTR = 320
NBLK = 16
GROUPS = ((0, 3), (3, 4), (4, 12), (12, 16))
PER_GROUP = 17


def column_of(row):
    return jnp.transpose(jnp.broadcast_to(row, (B, B)))


def kernel(
    tok_hbm, seg_ref, ord_ref, cnt_ref, g1_ref, g2_ref,
    wq, wk, wv, wo, wg, wu, wd,
    out_ref,
    W, X, wqkv, q, k, v, att, ATT, SND, tokc, tokl,
    RS1, RB1, AGB, LHS, SS, ACC, H, RS2, RB2, FIN, FSND, segf, ordf, ordm,
    lsem, wsend, wrecv, z_send, z_recv, dsend, drecv,
):
    z = lax.axis_index("dp")
    j = lax.axis_index("fsdp")
    c = lax.axis_index("tensor")
    x = j // NY
    y = lax.rem(j, NY)
    xp = lax.rem(x + 1, NX)
    xm = lax.rem(x + NX - 1, NX)
    yp = lax.rem(y + 1, NY)
    ym = lax.rem(y + NY - 1, NY)
    zp = lax.rem(z + 1, NZ)
    zm = lax.rem(z + NZ - 1, NZ)
    dev_xp = {"fsdp": xp * NY + y}
    dev_xm = {"fsdp": xm * NY + y}
    dev_yp = {"fsdp": x * NY + yp}
    dev_ym = {"fsdp": x * NY + ym}
    dev_zp = {"dp": zp}
    dev_zm = {"dp": zm}
    dev_c = {"tensor": 1 - c}

    own = W.at[x, y, c]
    local = []
    for i, (ref) in enumerate((wq, wk, wv, wo)):
        local.append(pltpu.make_async_copy(ref, own.at[i], lsem.at[i]))
    for i in range(4):
        local.append(pltpu.make_async_copy(wg.at[:, pl.ds(i * B, B)], own.at[4 + i], lsem.at[4 + i]))
    for i in range(4):
        local.append(pltpu.make_async_copy(wu.at[:, pl.ds(i * B, B)], own.at[8 + i], lsem.at[8 + i]))
    for i in range(4):
        local.append(pltpu.make_async_copy(wd.at[pl.ds(i * B, B), :], own.at[12 + i], lsem.at[12 + i]))
    for i in range(3):
        local[i].start()
    tok = [
        pltpu.make_async_copy(
            tok_hbm.at[pl.ds(i * 256, 256), :], X.at[pl.ds(i * 256, 256), :], lsem.at[16 + i]
        )
        for i in range(8)
    ]
    for i in range(8):
        tok[i].start()
    for i in range(3, 16):
        local[i].start()
    tc = pltpu.make_async_copy(
        tok_hbm.at[:, pl.ds(pl.multiple_of(z * 256, 256), 256)], tokc, lsem.at[24]
    )
    tc.start()

    barrier = pltpu.get_barrier_semaphore()
    for dev in (dev_xp, dev_xm, dev_yp, dev_ym, dev_zp, dev_zm, dev_c):
        pl.semaphore_signal(barrier, inc=1, device_id=dev, device_id_type=pl.DeviceIdType.MESH)
    pl.semaphore_wait(barrier, 7)

    sent = []

    def remote(src, dst, ss, rs, dev):
        return pltpu.make_async_remote_copy(
            src_ref=src, dst_ref=dst, send_sem=ss, recv_sem=rs,
            device_id=dev, device_id_type=pl.DeviceIdType.MESH,
        )

    def go(cp):
        cp.start()
        sent.append(cp)

    def plan(g):
        a, b = GROUPS[g]
        nb = pl.ds(a, b - a)

        def cp(i, idx, dev):
            ref = W.at[idx]
            n = g * PER_GROUP + i
            return remote(ref, ref, wsend.at[n], wrecv.at[n], dev)

        alla = pl.ds(0, 64)
        allb = pl.ds(64, 64)
        full = pl.ds(0, 4)
        lo, hi = pl.ds(0, 2), pl.ds(2, 2)
        copies = [
            cp(0, (x, y, c, nb, alla), dev_xp),
            cp(1, (x, y, c, nb, alla), dev_xm),
            cp(2, (x, y, c, nb, allb), dev_yp),
            cp(3, (x, y, c, nb, allb), dev_ym),
            cp(4, (xm, y, c, nb, pl.ds(0, 32)), dev_xp),
            cp(5, (xp, y, c, nb, pl.ds(32, 32)), dev_xm),
            cp(6, (x, ym, c, nb, pl.ds(64, 32)), dev_yp),
            cp(7, (x, yp, c, nb, pl.ds(96, 32)), dev_ym),
            cp(8, (full, y, c, nb, alla), dev_yp),
            cp(9, (full, y, c, nb, alla), dev_ym),
            cp(10, (x, full, c, nb, allb), dev_xp),
            cp(11, (x, full, c, nb, allb), dev_xm),
            cp(12, (lo, ym, c, nb, alla), dev_yp),
            cp(13, (hi, yp, c, nb, alla), dev_ym),
            cp(14, (xm, lo, c, nb, allb), dev_xp),
            cp(15, (xp, hi, c, nb, allb), dev_xm),
        ]
        if g > 0:
            copies.append(cp(16, (full, full, c, nb), dev_c))

        def stage(s):
            if s == 0:
                for i in range(a, b):
                    local[i].wait()
            elif s <= 4:
                for i in range(4 * s - 4, 4 * s):
                    copies[i].wait_recv()
            if s < 4:
                for i in range(4 * s, 4 * s + 4):
                    go(copies[i])
            elif s == 4 and g > 0:
                go(copies[16])
            elif s == 5:
                copies[16].wait_recv()

        return stage

    gathers = [plan(g) for g in range(4)]

    segf[...] = seg_ref[...].astype(F32)
    order = ord_ref[...].astype(F32)
    ordf[...] = order
    rank = lax.broadcasted_iota(jnp.int32, (NBLK, B), 0) * B + lax.broadcasted_iota(
        jnp.int32, (NBLK, B), 1
    )
    ordm[...] = jnp.where(rank < cnt_ref[j], order, -1.0)
    gain1 = jnp.concatenate([g1_ref[pl.ds(i, 1), :] for i in range(NBLK)], axis=1)

    def norm_chunk(i):
        tok[i].wait()

        def body(r, _):
            rows = pl.ds(pl.multiple_of(i * 256 + r * 16, 16), 16)
            f = X[rows, :].astype(F32)
            inv = lax.rsqrt(jnp.mean(f * f, axis=-1, keepdims=True) + 1e-05)
            X[rows, :] = (f * inv * gain1).astype(BF16)
            return 0

        lax.fori_loop(0, 16, body, 0, unroll=2)

    gathers[0](0)
    norm_chunk(0)
    norm_chunk(1)
    gathers[0](1)
    norm_chunk(2)
    norm_chunk(3)
    gathers[0](2)
    norm_chunk(4)
    norm_chunk(5)
    norm_chunk(6)
    norm_chunk(7)
    gathers[0](3)
    gathers[1](0)
    gathers[0](4)
    gathers[2](0)

    def fill(jj, _):
        for b in range(3):
            wqkv[pl.ds(pl.multiple_of(jj * B, B), B), pl.ds(b * B, B)] = W[
                jj // NY, lax.rem(jj, NY), c, b
            ]
        return 0

    lax.fori_loop(0, 16, fill, 0)

    def qkv_tile(m, _):
        rows = pl.ds(pl.multiple_of(m * 256, 256), 256)
        r = jnp.dot(X[rows, :], wqkv[...], preferred_element_type=F32).astype(BF16)
        q[rows, :] = r[:, 0:B]
        k[rows, :] = r[:, B : 2 * B]
        v[rows, :] = r[:, 2 * B : 3 * B]
        return 0

    lax.fori_loop(0, 2, qkv_tile, 0)
    gathers[1](1)
    lax.fori_loop(2, 4, qkv_tile, 0)
    gathers[1](2)
    gathers[2](1)
    lax.fori_loop(4, 8, qkv_tile, 0)
    gathers[1](3)
    gathers[2](2)

    scale = 1.0 / math.sqrt(B)

    def att_block(i, _):
        st = jnp.maximum(i - 4, 0)
        qrows = pl.ds(pl.multiple_of(i * B, B), B)
        krows = pl.ds(pl.multiple_of(st * B, B), 5 * B)
        s = (
            lax.dot_general(
                q[qrows, :], k[krows, :], (((1,), (1,)), ((), ())), preferred_element_type=F32
            )
            * scale
        )
        segq = column_of(segf[pl.ds(i, 1), :])
        segq = jnp.concatenate([segq] * 5, axis=1)
        segk = jnp.concatenate([segf[pl.ds(st + t, 1), :] for t in range(5)], axis=1)
        diff = lax.broadcasted_iota(jnp.int32, (B, 5 * B), 0) - lax.broadcasted_iota(
            jnp.int32, (B, 5 * B), 1
        )
        allowed = (segq == segk) & (diff >= (st - i) * B)
        s = jnp.where(allowed, s, -1e30)
        e = jnp.exp(s - jnp.max(s, axis=-1, keepdims=True))
        p = (e * (1.0 / jnp.sum(e, axis=-1, keepdims=True))).astype(BF16)
        att[qrows, :] = jnp.dot(p, v[krows, :], preferred_element_type=F32).astype(BF16)
        return 0

    lax.fori_loop(0, 8, att_block, 0)
    gathers[1](4)
    lax.fori_loop(8, 16, att_block, 0)

    lane = lax.broadcasted_iota(jnp.int32, (B, B), 1).astype(F32)
    sub = lax.broadcasted_iota(jnp.int32, (B, B), 0).astype(F32)

    def one_hot(rb):
        col = column_of(ordf[pl.ds(rb, 1), :])
        return jnp.concatenate(
            [jnp.where(col == lane + (B * u), 1.0, 0.0).astype(BF16) for u in range(NBLK)], axis=1
        )

    def pick_other(t, _):
        oh = one_hot((1 - c) * 5 + t)
        SND[pl.ds(pl.multiple_of(t * B, B), B), :] = jnp.dot(
            oh, att[...], preferred_element_type=F32
        ).astype(BF16)
        return 0

    lax.fori_loop(0, 5, pick_other, 0)
    swap = remote(SND, ATT.at[c], dsend.at[0], drecv.at[0], dev_c)
    go(swap)
    tc.wait()

    def pick_own(t, _):
        oh = one_hot(c * 5 + t)
        rows = pl.ds(pl.multiple_of(t * B, B), B)
        ATT[c, rows, :] = jnp.dot(oh, att[...], preferred_element_type=F32).astype(BF16)
        tokl[rows, :] = jnp.dot(oh, tokc[...], preferred_element_type=F32).astype(BF16)
        return 0

    lax.fori_loop(0, 5, pick_own, 0)
    gathers[1](5)
    swap.wait_recv()

    def w_index(zs):
        return zs // 2, 2 * lax.rem(zs, 2)

    def ring_copy(base, src, dst, d, s, h):
        n = base + (d * 4 + s) * 2 + h
        return remote(src, dst, z_send.at[n], z_recv.at[n], dev_zp if d == 0 else dev_zm)

    def reduce_ring(base, R, RB, partial, finish, extras):
        copies = {}
        for d in (0, 1):
            far = lax.rem(z + 4, NZ)
            RB[d] = partial(far, d).astype(BF16)
            copies[d, 0, d] = ring_copy(base, RB.at[d], R.at[d, 0, d], d, 0, d)
            go(copies[d, 0, d])
        for s in (1, 2, 3):
            order_h = ((0, 1), (1, 0), (0, 0), (1, 1)) if s == 1 else ((0, 0), (1, 1), (0, 1), (1, 0))
            if s > 1:
                order_h = ((0, 1), (1, 0), (0, 0), (1, 1))
            for d, h in order_h:
                dest = lax.rem(z + 4 - s, NZ) if d == 0 else lax.rem(z + 4 + s, NZ)
                part = partial(dest, h)
                slot = R.at[d, s - 1, h]
                if (d, s - 1, h) in copies:
                    copies[d, s - 1, h].wait_recv()
                    part = part + slot[...].astype(F32)
                slot[...] = part.astype(BF16)
                copies[d, s, h] = ring_copy(base, slot, R.at[d, s, h], d, s, h)
                go(copies[d, s, h])
            for f in extras.get(s, ()):
                f()
        for h in (1, 0):
            part = partial(z, h)
            copies[0, 3, h].wait_recv()
            copies[1, 3, h].wait_recv()
            finish(h, part + R[0, 3, h].astype(F32) + R[1, 3, h].astype(F32))

    def rows_of(h):
        return pl.ds(h * QTR, QTR)

    def head_partial(zd, h):
        xw, yw = w_index(zd)
        rhs = jnp.concatenate(
            [
                jnp.concatenate([W[xw, yw + e, cc, 3] for e in range(2)], axis=1)
                for cc in range(2)
            ],
            axis=0,
        )
        lhs = jnp.concatenate([ATT[0, rows_of(h), :], ATT[1, rows_of(h), :]], axis=1)
        return jnp.dot(lhs, rhs, preferred_element_type=F32)

    def head_finish(h, total):
        AGB[z, rows_of(h), :] = (tokl[rows_of(h), :].astype(F32) + total).astype(BF16)
        for d in (0, 1):
            go(ag_copy(d, 0, h))

    ag = {}

    def ag_copy(d, s, h):
        if (d, s, h) not in ag:
            src = lax.rem(z + NZ - s, NZ) if d == 0 else lax.rem(z + s, NZ)
            ref = AGB.at[src, rows_of(h)]
            ag[d, s, h] = ring_copy(16, ref, ref, d, s, h)
        return ag[d, s, h]

    reduce_ring(
        0, RS1, RB1, head_partial, head_finish,
        {
            1: (lambda: gathers[2](3),),
            2: (lambda: gathers[3](0),),
            3: (lambda: gathers[2](4), lambda: gathers[3](1)),
        },
    )

    def ff_in(zs, h, first):
        xw, yw = w_index(zs)
        rows = rows_of(h)
        f = AGB[zs, rows, :].astype(F32)
        sq = f * f
        sq = sq[:, :B] + sq[:, B:]
        SS[rows, :] = sq if first else SS[rows, :] + sq
        gain = jnp.concatenate([g2_ref[pl.ds(2 * zs + e, 1), :] for e in range(2)], axis=1)
        LHS[...] = (f * gain).astype(BF16)

        def body(n, _):
            cc = n // 2
            blk = 4 + 4 * lax.rem(n, 2)
            rhs = jnp.concatenate(
                [
                    jnp.concatenate([W[xw, yw + e, cc, blk + b] for b in range(4)], axis=1)
                    for e in range(2)
                ],
                axis=0,
            )
            prod = jnp.dot(LHS[...], rhs, preferred_element_type=F32)
            if first:
                ACC[n, rows, :] = prod
            else:
                ACC[n, rows, :] = ACC[n, rows, :] + prod
            return 0

        lax.fori_loop(0, 4, body, 0)

    gathers[3](2)
    gathers[2](5)
    ff_in(z, 1, True)
    ff_in(z, 0, True)
    for s in range(4):
        got = []
        for h in (1, 0):
            for d in (0, 1):
                if s == 3 and h != d:
                    continue
                ag_copy(d, s, h).wait_recv()
                got.append((d, h))
                if s < 2 or (s == 2 and h == d):
                    go(ag_copy(d, s + 1, h))
        if s == 0:
            gathers[3](3)
        if s == 1:
            gathers[3](4)
        for d, h in got:
            ff_in(lax.rem(z + NZ - 1 - s, NZ) if d == 0 else lax.rem(z + 1 + s, NZ), h, False)

    def act(r, _):
        rows = pl.ds(pl.multiple_of(r * 32, 32), 32)
        inv = lax.rsqrt(jnp.sum(SS[rows, :], axis=-1, keepdims=True) * (1.0 / D) + 1e-05)
        for cc in range(2):
            g = ACC[2 * cc, rows, :] * inv
            u = ACC[2 * cc + 1, rows, :] * inv
            H[rows, pl.ds(cc * 512, 512)] = (g / (1.0 + jnp.exp(-g)) * u).astype(BF16)
        return 0

    lax.fori_loop(0, HALF // 32, act, 0)
    gathers[3](5)

    def ff_partial(zd, h):
        xw, yw = w_index(zd)
        rhs = jnp.concatenate(
            [
                jnp.concatenate([W[xw, yw + e, cc, 12 + b] for e in range(2)], axis=1)
                for cc in range(2)
                for b in range(4)
            ],
            axis=0,
        )
        return jnp.dot(H[rows_of(h), :], rhs, preferred_element_type=F32)

    def ff_finish(h, total):
        fin = (AGB[z, rows_of(h), :].astype(F32) + total).astype(BF16)
        FIN[c, rows_of(h), :] = jnp.where(c == 0, fin[:, :B], fin[:, B:])
        FSND[rows_of(h), :] = jnp.where(c == 0, fin[:, B:], fin[:, :B])

    reduce_ring(32, RS2, RB2, ff_partial, ff_finish, {})
    swap2 = remote(FSND, FIN.at[c], dsend.at[1], drecv.at[1], dev_c)
    go(swap2)
    swap2.wait_recv()

    ones = jnp.ones((HALF, B), BF16)

    def put(t, _):
        rows = pl.ds(pl.multiple_of(t * B, B), B)
        base = (t * B).astype(F32)
        acc = jnp.zeros((B, 2 * B), F32)
        for half in range(2):
            oh = jnp.concatenate(
                [
                    jnp.where(ordm[pl.ds(half * 5 + u, 1), :] == sub + base, 1.0, 0.0).astype(BF16)
                    for u in range(5)
                ],
                axis=1,
            )
            acc = acc + jnp.dot(
                oh, jnp.concatenate([FIN[half], ones], axis=1), preferred_element_type=F32
            )
        old = tokc[rows, :]
        old = jnp.where(c == 0, old[:, :B], old[:, B:])
        out_ref[rows, :] = jnp.where(acc[:, B:] > 0.5, acc[:, :B], old.astype(F32)).astype(BF16)
        return 0

    lax.fori_loop(0, NBLK, put, 0)
    for cp in sent:
        cp.wait_send()


def body(
    tokens, segment_ids, row_order, row_counts, first_gain, second_gain,
    query_weight, key_weight, value_weight, output_weight, gate_weight, up_weight, down_weight,
):
    vm = pl.BlockSpec(memory_space=pltpu.VMEM)
    anyspace = pl.BlockSpec(memory_space=pl.ANY)
    smem = pl.BlockSpec(memory_space=pltpu.SMEM)
    return pl.pallas_call(
        kernel,
        out_shape=jax.ShapeDtypeStruct((ROWS, B), BF16),
        in_specs=[anyspace, vm, vm, smem, vm, vm] + [anyspace] * 7,
        out_specs=vm,
        scratch_shapes=[
            pltpu.VMEM((NX, NY, 2, NBLK, B, B), BF16),
            pltpu.VMEM((ROWS, D), BF16),
            pltpu.VMEM((D, 3 * B), BF16),
            pltpu.VMEM((ROWS, B), BF16),
            pltpu.VMEM((ROWS, B), BF16),
            pltpu.VMEM((ROWS, B), BF16),
            pltpu.VMEM((ROWS, B), BF16),
            pltpu.VMEM((2, HALF, B), BF16),
            pltpu.VMEM((HALF, B), BF16),
            pltpu.VMEM((ROWS, 2 * B), BF16),
            pltpu.VMEM((HALF, 2 * B), BF16),
            pltpu.VMEM((2, 4, 2, QTR, 2 * B), BF16),
            pltpu.VMEM((2, QTR, 2 * B), BF16),
            pltpu.VMEM((NZ, HALF, 2 * B), BF16),
            pltpu.VMEM((QTR, 2 * B), BF16),
            pltpu.VMEM((HALF, B), F32),
            pltpu.VMEM((4, HALF, 512), F32),
            pltpu.VMEM((HALF, 1024), BF16),
            pltpu.VMEM((2, 4, 2, QTR, 2 * B), BF16),
            pltpu.VMEM((2, QTR, 2 * B), BF16),
            pltpu.VMEM((2, HALF, B), BF16),
            pltpu.VMEM((HALF, B), BF16),
            pltpu.VMEM((NBLK, B), F32),
            pltpu.VMEM((NBLK, B), F32),
            pltpu.VMEM((NBLK, B), F32),
            pltpu.SemaphoreType.DMA((25,)),
            pltpu.SemaphoreType.DMA((4 * PER_GROUP,)),
            pltpu.SemaphoreType.DMA((4 * PER_GROUP,)),
            pltpu.SemaphoreType.DMA((48,)),
            pltpu.SemaphoreType.DMA((48,)),
            pltpu.SemaphoreType.DMA((2,)),
            pltpu.SemaphoreType.DMA((2,)),
        ],
        compiler_params=pltpu.CompilerParams(
            collective_id=0, has_side_effects=True, vmem_limit_bytes=66 * 1000 * 1000
        ),
        name="recursion_step",
    )(
        tokens,
        segment_ids.reshape(NBLK, B),
        row_order.reshape(NBLK, B),
        row_counts,
        first_gain.reshape(NBLK, B),
        second_gain.reshape(NBLK, B),
        query_weight, key_weight, value_weight, output_weight,
        gate_weight, up_weight, down_weight,
    )


def solution(mesh):
    weight = P("fsdp", ("dp", "tensor"))
    weight_t = P(("dp", "tensor"), "fsdp")
    in_specs = (
        P("fsdp", None), P("fsdp"), P("fsdp"), P(), P(), P(),
        weight, weight, weight, weight_t, weight, weight, weight_t,
    )
    return jax.shard_map(
        body, mesh=mesh, in_specs=in_specs, out_specs=weight, check_vma=False
    )
```

```python
import math

import jax
import jax.numpy as jnp
from jax import lax
from jax.experimental import pallas as pl
from jax.experimental.pallas import tpu as pltpu
from jax.sharding import PartitionSpec as P

F32 = jnp.float32
BF16 = jnp.bfloat16
NZ = 8
NX = 4
NY = 4
B = 128
ROWS = 2048
D = 2048
HALF = 640
QTR = 320
NBLK = 16
PIECE = 80
O_AT, G_AT, U_AT, D_AT, BLOCKS = 3, 11, 15, 19, 23
GROUPS = ((0, 3), (3, 11), (11, 19), (19, 23))
PER_GROUP = 29


def column_of(row):
    return jnp.transpose(jnp.broadcast_to(row, (B, B)))


def kernel(
    tok_hbm, seg_ref, ord_ref, cnt_ref, g1_ref, g2_ref,
    wq, wk, wv, wo, wg, wu, wd,
    out_ref,
    W, X, XN, q, k, v, att, OHP, PICK, A2, AGB, NRM, H, RS2, RB2, FIN, FSND, P1, LIVE,
    segf, ordf, ordm,
    lsem, wsend, wrecv, z_send, z_recv, dsend, drecv,
):
    z = lax.axis_index("dp")
    j = lax.axis_index("fsdp")
    c = lax.axis_index("tensor")
    x = j // NY
    y = lax.rem(j, NY)
    xp = lax.rem(x + 1, NX)
    xm = lax.rem(x + 3, NX)
    x2 = lax.rem(x + 2, NX)
    yp = lax.rem(y + 1, NY)
    ym = lax.rem(y + 3, NY)
    y2 = lax.rem(y + 2, NY)
    dev_xp = {"fsdp": xp * NY + y}
    dev_xm = {"fsdp": xm * NY + y}
    dev_yp = {"fsdp": x * NY + yp}
    dev_ym = {"fsdp": x * NY + ym}
    dev_c = {"tensor": 1 - c}

    def z_at(step):
        return lax.rem(z + step, NZ)

    def dev_z(step, other=0):
        if other:
            return {"dp": z_at(step), "tensor": 1 - c}
        return {"dp": z_at(step)}

    barrier = pltpu.get_barrier_semaphore()
    peers = [dev_xp, dev_xm, dev_yp, dev_ym, dev_c]
    peers += [dev_z(dz, other) for dz in range(1, NZ) for other in (0, 1)]
    for dev in peers:
        pl.semaphore_signal(barrier, inc=1, device_id=dev, device_id_type=pl.DeviceIdType.MESH)

    own = W.at[x, y, c]
    spots = [(wq, 0), (wk, 1), (wv, 2), (wo, O_AT + z)]
    spots += [(wg.at[:, pl.ds(i * B, B)], G_AT + i) for i in range(4)]
    spots += [(wu.at[:, pl.ds(i * B, B)], U_AT + i) for i in range(4)]
    spots += [(wd.at[pl.ds(i * B, B), :], D_AT + i) for i in range(4)]
    local = [pltpu.make_async_copy(ref, own.at[b], lsem.at[i]) for i, (ref, b) in enumerate(spots)]
    local_of = ((0, 3), (3, 4), (4, 12), (12, 16))
    for i in range(4):
        local[i].start()
    tok = [
        pltpu.make_async_copy(
            tok_hbm.at[pl.ds(i * 256, 256), :], X.at[pl.ds(i * 256, 256), :], lsem.at[16 + i]
        )
        for i in range(8)
    ]
    for i in range(8):
        tok[i].start()
    for i in range(4, 16):
        local[i].start()

    pl.semaphore_wait(barrier, len(peers))

    sent = []

    def remote(src, dst, ss, rs, dev):
        return pltpu.make_async_remote_copy(
            src_ref=src, dst_ref=dst, send_sem=ss, recv_sem=rs,
            device_id=dev, device_id_type=pl.DeviceIdType.MESH,
        )

    def go(cp):
        cp.start()
        sent.append(cp)

    def plan(g):
        a, b = GROUPS[g]
        nb = pl.ds(a, b - a)
        up, dn = pl.ds(0, 64), pl.ds(64, 64)
        full = pl.ds(0, 4)
        lo, hi = pl.ds(0, 2), pl.ds(2, 2)

        def cp(i, idx, dev):
            ref = W.at[idx]
            n = g * PER_GROUP + i
            return remote(ref, ref, wsend.at[n], wrecv.at[n], dev)

        copies = [
            ((x, y, c, nb, up), dev_xp),
            ((x, y, c, nb, up), dev_xm),
            ((x, y, c, nb, dn), dev_yp),
            ((x, y, c, nb, dn), dev_ym),
            ((xm, y, c, nb, pl.ds(0, 32)), dev_xp),
            ((xp, y, c, nb, pl.ds(32, 32)), dev_xm),
            ((x, ym, c, nb, pl.ds(64, 32)), dev_yp),
            ((x, yp, c, nb, pl.ds(96, 32)), dev_ym),
            ((full, y, c, nb, up), dev_yp),
            ((full, y, c, nb, up), dev_ym),
            ((x, full, c, nb, dn), dev_xp),
            ((x, full, c, nb, dn), dev_xm),
            ((lo, ym, c, nb, up), dev_yp),
            ((hi, yp, c, nb, up), dev_ym),
            ((xm, lo, c, nb, dn), dev_xp),
            ((xp, hi, c, nb, dn), dev_xm),
        ]
        pass_on = (
            ((x, y, c, nb),),
            ((xm, y, c, nb, up), (xp, y, c, nb, up), (x, ym, c, nb, dn), (x, yp, c, nb, dn)),
            ((x2, y, c, nb, up), (x, y2, c, nb, dn)),
            ((full, ym, c, nb, up), (full, yp, c, nb, up), (xm, full, c, nb, dn), (xp, full, c, nb, dn)),
            ((full, y2, c, nb, up), (x2, full, c, nb, dn)),
        )
        first = (16, 17, 21, 23, 27)
        made = {}

        def stage(s):
            if s == 5:
                for i in range(16, 29):
                    made[i].wait_recv()
                return
            if s == 0:
                for i in range(*local_of[g]):
                    if i != 3:
                        local[i].wait()
            else:
                for i in range(4 * s - 4, 4 * s):
                    made[i].wait_recv()
            if s < 4:
                for i in range(4 * s, 4 * s + 4):
                    made[i] = cp(i, *copies[i])
                    go(made[i])
            if g > 0:
                for e, idx in enumerate(pass_on[s]):
                    i = first[s] + e
                    made[i] = cp(i, idx, dev_c)
                    go(made[i])

        return stage

    gathers = [plan(g) for g in range(4)]

    gathers[0](0)
    local[3].wait()
    o_piece = own.at[O_AT + z]
    o_copies = [
        remote(o_piece, o_piece, z_send.at[dz], z_recv.at[dz], dev_z(dz)) for dz in range(1, NZ)
    ]
    for cp in o_copies:
        go(cp)

    segf[...] = seg_ref[...].astype(F32)
    order = ord_ref[...].astype(F32)
    ordf[...] = order
    rank = lax.broadcasted_iota(jnp.int32, (NBLK, B), 0) * B + lax.broadcasted_iota(
        jnp.int32, (NBLK, B), 1
    )
    ordm[...] = jnp.where(rank < cnt_ref[j], order, -1.0)
    gain1 = jnp.concatenate([g1_ref[pl.ds(i, 1), :] for i in range(NBLK)], axis=1)
    gain2 = jnp.concatenate([g2_ref[pl.ds(i, 1), :] for i in range(NBLK)], axis=1)

    def normed(data, gain):
        f = data.astype(F32)
        inv = lax.rsqrt(jnp.mean(f * f, axis=-1, keepdims=True) + 1e-05)
        return (f * inv * gain).astype(BF16)

    def norm_chunk(i):
        tok[i].wait()

        def body(r, _):
            rows = pl.ds(pl.multiple_of(i * 256 + r * 16, 16), 16)
            XN[rows, :] = normed(X[rows, :], gain1)
            return 0

        lax.fori_loop(0, 16, body, 0, unroll=4)

    lane = lax.broadcasted_iota(jnp.int32, (B, B), 1).astype(F32)
    sub = lax.broadcasted_iota(jnp.int32, (B, B), 0).astype(F32)

    def one_hot(t, _):
        rows = pl.ds(pl.multiple_of(t * B, B), B)
        col = column_of(ordf[pl.ds(t, 1), :])
        for u in range(NBLK):
            OHP[rows, pl.ds(u * B, B)] = jnp.where(col == lane + (B * u), 1.0, 0.0).astype(BF16)
        return 0

    norm_chunk(0)
    norm_chunk(1)
    norm_chunk(2)
    gathers[0](1)
    norm_chunk(3)
    norm_chunk(4)
    gathers[0](2)
    norm_chunk(5)
    norm_chunk(6)
    norm_chunk(7)
    lax.fori_loop(0, 10, one_hot, 0)
    gathers[0](3)
    for cp in o_copies:
        cp.wait_recv()
    gathers[1](0)
    gathers[0](4)

    def blocks(cc, b, count):
        return jnp.concatenate(
            [
                jnp.concatenate([W[i // NY, i % NY, cc, b + e] for e in range(count)], axis=1)
                for i in range(16)
            ],
            axis=0,
        )

    def qkv_tile(m, _):
        rows = pl.ds(pl.multiple_of(m * 256, 256), 256)
        r = jnp.dot(XN[rows, :], blocks(c, 0, 3), preferred_element_type=F32).astype(BF16)
        q[rows, :] = r[:, 0:B]
        k[rows, :] = r[:, B : 2 * B]
        v[rows, :] = r[:, 2 * B : 3 * B]
        return 0

    lax.fori_loop(0, 5, qkv_tile, 0)
    gathers[1](1)
    gathers[2](0)
    lax.fori_loop(5, 8, qkv_tile, 0)

    scale = 1.0 / math.sqrt(B)

    def att_block(i, _):
        st = jnp.maximum(i - 4, 0)
        qrows = pl.ds(pl.multiple_of(i * B, B), B)
        krows = pl.ds(pl.multiple_of(st * B, B), 5 * B)
        s = (
            lax.dot_general(
                q[qrows, :], k[krows, :], (((1,), (1,)), ((), ())), preferred_element_type=F32
            )
            * scale
        )
        segq = column_of(segf[pl.ds(i, 1), :])
        segq = jnp.concatenate([segq] * 5, axis=1)
        segk = jnp.concatenate([segf[pl.ds(st + t, 1), :] for t in range(5)], axis=1)
        diff = lax.broadcasted_iota(jnp.int32, (B, 5 * B), 0) - lax.broadcasted_iota(
            jnp.int32, (B, 5 * B), 1
        )
        allowed = (segq == segk) & (diff >= (st - i) * B)
        s = jnp.where(allowed, s, -1e30)
        e = jnp.exp(s - jnp.max(s, axis=-1, keepdims=True))
        p = (e * (1.0 / jnp.sum(e, axis=-1, keepdims=True))).astype(BF16)
        att[qrows, :] = jnp.dot(p, v[krows, :], preferred_element_type=F32).astype(BF16)
        return 0

    lax.fori_loop(0, 4, att_block, 0, unroll=2)
    gathers[1](2)
    lax.fori_loop(4, 10, att_block, 0, unroll=2)
    gathers[2](1)
    lax.fori_loop(10, 16, att_block, 0, unroll=2)

    def pick(t, _):
        rows = pl.ds(pl.multiple_of(t * 256, 256), 256)
        PICK[rows, :] = jnp.dot(OHP[rows, :], att[...], preferred_element_type=F32).astype(BF16)
        return 0

    lax.fori_loop(0, 5, pick, 0)

    def piece_rows(zs, cc):
        return pl.ds(pl.multiple_of(cc * HALF + zs * PIECE, 16), PIECE)

    spread = []
    for dz in (4, 3, 5, 2, 6, 1, 7, 0):
        for other in (0, 1):
            if dz == 0 and other == 0:
                continue
            cc = 1 - c if other else c
            n = 8 + dz * 2 + other
            dev = dev_z(dz, other) if dz else dev_c
            spread.append(
                remote(
                    PICK.at[piece_rows(z_at(dz), cc)], A2.at[2 * z + c],
                    z_send.at[n], z_recv.at[n], dev,
                )
            )
            go(spread[-1])
    A2[2 * z + c] = PICK[piece_rows(z, c), :]

    def row_tokens(n, _):
        cols = pl.ds(pl.multiple_of(n * 256, 256), 256)
        AGB[z, :, cols] = jnp.dot(
            OHP[piece_rows(z, c), :], X[:, cols], preferred_element_type=F32
        ).astype(BF16)
        return 0

    lax.fori_loop(0, 8, row_tokens, 0)

    def put_hot(t, _):
        rows = pl.ds(pl.multiple_of(t * B, B), B)
        base = (t * B).astype(F32)
        for u in range(10):
            XN[rows, pl.ds(u * B, B)] = jnp.where(
                ordm[pl.ds(u, 1), :] == sub + base, 1.0, 0.0
            ).astype(BF16)
        return 0

    lax.fori_loop(0, 8, put_hot, 0)
    gathers[1](3)
    gathers[2](2)
    lax.fori_loop(8, 16, put_hot, 0)
    ones = jnp.ones((2 * HALF, B), BF16)

    def live(t, _):
        rows = pl.ds(pl.multiple_of(t * 256, 256), 256)
        LIVE[rows, :] = jnp.dot(
            XN[rows, pl.ds(0, 2 * HALF)], ones, preferred_element_type=F32
        ).astype(BF16)
        return 0

    lax.fori_loop(0, 8, live, 0)
    gathers[1](4)
    for cp in spread:
        cp.wait_recv()
    gathers[1](5)

    def w_index(n):
        return n // 2, 2 * lax.rem(n, 2)

    def ring_copy(base, src, dst, d, s, h):
        n = base + (d * 4 + s) * 2 + h
        return remote(src, dst, z_send.at[n], z_recv.at[n], dev_z(1) if d == 0 else dev_z(7))

    ag = {}

    def ag_copy(d, s, h):
        if (d, s, h) not in ag:
            src = z_at(NZ - s) if d == 0 else z_at(s)
            ref = AGB.at[src, :, pl.ds(h * 1024, 1024)]
            ag[d, s, h] = ring_copy(24, ref, ref, d, s, h)
        return ag[d, s, h]

    def out_proj(n, _):
        xw, yw = w_index(n)
        cols = pl.ds(pl.multiple_of(n * 256, 256), 256)
        rhs = jnp.concatenate(
            [
                jnp.concatenate([W[xw, yw + e, hh % 2, O_AT + hh // 2] for e in range(2)], axis=1)
                for hh in range(16)
            ],
            axis=0,
        )
        lhs = jnp.concatenate([A2[hh] for hh in range(16)], axis=1)
        total = jnp.dot(lhs, rhs, preferred_element_type=F32)
        AGB[z, :, cols] = (AGB[z, :, cols].astype(F32) + total).astype(BF16)
        return 0

    for h in (0, 1):
        lax.fori_loop(4 * h, 4 * h + 4, out_proj, 0)
        for d in (0, 1):
            go(ag_copy(d, 0, h))

    def prepare(i, zs):
        for r in range(0, PIECE, 16):
            NRM[pl.ds(i * PIECE + r, 16), :] = normed(AGB[zs, pl.ds(r, 16), :], gain2)

    def ff_in(sources):
        count = len(sources)

        def body(n, _):
            cc = n // 2
            e = 2 * lax.rem(n, 2)
            lhs = NRM[pl.ds(0, count * PIECE), :]
            g = jnp.dot(lhs, blocks(cc, G_AT + e, 2), preferred_element_type=F32)
            u = jnp.dot(lhs, blocks(cc, U_AT + e, 2), preferred_element_type=F32)
            hid = (g / (1.0 + jnp.exp(-g)) * u).astype(BF16)
            cols = pl.ds(pl.multiple_of(n * 256, 256), 256)
            for i, zs in enumerate(sources):
                H[pl.ds(pl.multiple_of(zs * PIECE, 16), PIECE), cols] = hid[
                    i * PIECE : (i + 1) * PIECE
                ]
            return 0

        lax.fori_loop(0, 4, body, 0)

    def receive(s):
        for h in (0, 1):
            for d in (0, 1):
                if s == 3 and h != d:
                    continue
                ag_copy(d, s, h).wait_recv()
                if s < 2 or (s == 2 and h == d):
                    go(ag_copy(d, s + 1, h))

    prepare(0, z)
    receive(0)
    prepare(1, z_at(1))
    prepare(2, z_at(7))
    gathers[2](3)
    gathers[3](0)
    receive(1)
    gathers[2](4)
    gathers[3](1)
    gathers[2](5)
    ff_in([z, z_at(1), z_at(7)])
    gathers[3](2)
    prepare(0, z_at(2))
    prepare(1, z_at(6))
    receive(2)
    ff_in([z_at(2), z_at(6)])
    gathers[3](3)
    prepare(0, z_at(3))
    prepare(1, z_at(5))
    ff_in([z_at(3), z_at(5)])
    receive(3)
    prepare(0, z_at(4))
    ff_in([z_at(4)])
    gathers[3](4)
    gathers[3](5)

    def rows_of(h):
        return pl.ds(h * QTR, QTR)

    def partial(zd, h):
        xw, yw = w_index(zd)
        rhs = jnp.concatenate(
            [
                jnp.concatenate([W[xw, yw + e, cc, D_AT + b] for e in range(2)], axis=1)
                for cc in range(2)
                for b in range(4)
            ],
            axis=0,
        )
        return jnp.dot(H[rows_of(h), :], rhs, preferred_element_type=F32)

    copies = {}
    for d in (0, 1):
        RB2[d] = partial(z_at(4), d).astype(BF16)
        copies[d, 0, d] = ring_copy(40, RB2.at[d], RS2.at[d, 0, d], d, 0, d)
        go(copies[d, 0, d])
    for s in (1, 2, 3):
        for d, h in ((0, 1), (1, 0), (0, 0), (1, 1)):
            part = partial(z_at(4 - s) if d == 0 else z_at(4 + s), h)
            slot = RS2.at[d, s - 1, h]
            if (d, s - 1, h) in copies:
                copies[d, s - 1, h].wait_recv()
                part = part + slot[...].astype(F32)
            slot[...] = part.astype(BF16)
            copies[d, s, h] = ring_copy(40, slot, RS2.at[d, s, h], d, s, h)
            go(copies[d, s, h])
    mine = pl.ds(pl.multiple_of(z * 256, 256), 256)
    for h in (1, 0):
        total = partial(z, h)
        copies[0, 3, h].wait_recv()
        copies[1, 3, h].wait_recv()
        total = total + RS2[0, 3, h].astype(F32) + RS2[1, 3, h].astype(F32)
        carried = jnp.concatenate([AGB[4 * h + i, :, mine] for i in range(4)], axis=0)
        fin = (carried.astype(F32) + total).astype(BF16)
        FIN[c, rows_of(h), :] = jnp.where(c == 0, fin[:, :B], fin[:, B:])
        FSND[rows_of(h), :] = jnp.where(c == 0, fin[:, B:], fin[:, :B])
    swap = remote(FSND, FIN.at[c], dsend.at[0], drecv.at[0], dev_c)
    go(swap)

    def put_own(t, _):
        rows = pl.ds(pl.multiple_of(t * 256, 256), 256)
        P1[rows, :] = jnp.dot(
            XN[rows, pl.ds(pl.multiple_of(c * HALF, B), HALF)], FIN[c], preferred_element_type=F32
        ).astype(BF16)
        return 0

    lax.fori_loop(0, 8, put_own, 0)
    swap.wait_recv()
    cols = pl.ds(pl.multiple_of((2 * z + c) * B, B), B)

    def put(t, _):
        rows = pl.ds(pl.multiple_of(t * 256, 256), 256)
        part = jnp.dot(
            XN[rows, pl.ds(pl.multiple_of((1 - c) * HALF, B), HALF)], FIN[1 - c],
            preferred_element_type=F32,
        )
        value = part + P1[rows, :].astype(F32)
        old = X[rows, cols].astype(F32)
        out_ref[rows, :] = jnp.where(LIVE[rows, :].astype(F32) > 0.5, value, old).astype(BF16)
        return 0

    lax.fori_loop(0, 8, put, 0)
    for cp in sent:
        cp.wait_send()


def body(
    tokens, segment_ids, row_order, row_counts, first_gain, second_gain,
    query_weight, key_weight, value_weight, output_weight, gate_weight, up_weight, down_weight,
):
    vm = pl.BlockSpec(memory_space=pltpu.VMEM)
    anyspace = pl.BlockSpec(memory_space=pl.ANY)
    smem = pl.BlockSpec(memory_space=pltpu.SMEM)
    return pl.pallas_call(
        kernel,
        out_shape=jax.ShapeDtypeStruct((ROWS, B), BF16),
        in_specs=[anyspace, vm, vm, smem, vm, vm] + [anyspace] * 7,
        out_specs=vm,
        scratch_shapes=[
            pltpu.VMEM((NX, NY, 2, BLOCKS, B, B), BF16),
            pltpu.VMEM((ROWS, D), BF16),
            pltpu.VMEM((ROWS, D), BF16),
            pltpu.VMEM((ROWS, B), BF16),
            pltpu.VMEM((ROWS, B), BF16),
            pltpu.VMEM((ROWS, B), BF16),
            pltpu.VMEM((ROWS, B), BF16),
            pltpu.VMEM((2 * HALF, ROWS), BF16),
            pltpu.VMEM((2 * HALF, B), BF16),
            pltpu.VMEM((16, PIECE, B), BF16),
            pltpu.VMEM((NZ, PIECE, D), BF16),
            pltpu.VMEM((3 * PIECE, D), BF16),
            pltpu.VMEM((HALF, 1024), BF16),
            pltpu.VMEM((2, 4, 2, QTR, 2 * B), BF16),
            pltpu.VMEM((2, QTR, 2 * B), BF16),
            pltpu.VMEM((2, HALF, B), BF16),
            pltpu.VMEM((HALF, B), BF16),
            pltpu.VMEM((ROWS, B), BF16),
            pltpu.VMEM((ROWS, B), BF16),
            pltpu.VMEM((NBLK, B), F32),
            pltpu.VMEM((NBLK, B), F32),
            pltpu.VMEM((NBLK, B), F32),
            pltpu.SemaphoreType.DMA((24,)),
            pltpu.SemaphoreType.DMA((4 * PER_GROUP,)),
            pltpu.SemaphoreType.DMA((4 * PER_GROUP,)),
            pltpu.SemaphoreType.DMA((56,)),
            pltpu.SemaphoreType.DMA((56,)),
            pltpu.SemaphoreType.DMA((1,)),
            pltpu.SemaphoreType.DMA((1,)),
        ],
        compiler_params=pltpu.CompilerParams(
            collective_id=0, has_side_effects=True, vmem_limit_bytes=67 * 1000 * 1000
        ),
        name="recursion_step",
    )(
        tokens,
        segment_ids.reshape(NBLK, B),
        row_order.reshape(NBLK, B),
        row_counts,
        first_gain.reshape(NBLK, B),
        second_gain.reshape(NBLK, B),
        query_weight, key_weight, value_weight, output_weight,
        gate_weight, up_weight, down_weight,
    )


def solution(mesh):
    weight = P("fsdp", ("dp", "tensor"))
    weight_t = P(("dp", "tensor"), "fsdp")
    in_specs = (
        P("fsdp", None), P("fsdp"), P("fsdp"), P(), P(), P(),
        weight, weight, weight, weight_t, weight, weight, weight_t,
    )
    return jax.shard_map(
        body, mesh=mesh, in_specs=in_specs, out_specs=weight, check_vma=False
    )
```

```python
import math

import jax
import jax.numpy as jnp
from jax import lax
from jax.experimental import pallas as pl
from jax.experimental.pallas import tpu as pltpu
from jax.sharding import PartitionSpec as P

F32 = jnp.float32
BF16 = jnp.bfloat16
NZ = 8
NX = 4
NY = 4
B = 128
ROWS = 2048
D = 2048
HALF = 640
QTR = 320
NBLK = 16
PIECE = 80
O_AT, G_AT, U_AT, D_AT, BLOCKS = 3, 11, 15, 19, 23
SENDS = 96
SLOT = {0: 0, 1: 1, -1: 2, 2: 3, -2: 4, 3: 5, -3: 6, 4: 7, -4: 7}
STEP_OF_SLOT = (0, 1, 7, 2, 6, 3, 5, 4)


def column_of(row):
    return jnp.transpose(jnp.broadcast_to(row, (B, B)))


def kernel(
    tok_hbm, seg_ref, ord_ref, cnt_ref, g1_ref, g2_ref,
    wq, wk, wv, wo, wg, wu, wd,
    out_ref,
    W, X, XN, q, k, v, att, OHP, PICK, A2, AGB, NRM, H, RS2, RB2, FIN, FSND, P1, LIVE, OUT,
    segf, ordf, ordm,
    lsem, ssem, wrecv, z_recv,
):
    z = lax.axis_index("dp")
    j = lax.axis_index("fsdp")
    c = lax.axis_index("tensor")
    x = j // NY
    y = lax.rem(j, NY)
    xp = lax.rem(x + 1, NX)
    xm = lax.rem(x + 3, NX)
    x2 = lax.rem(x + 2, NX)
    yp = lax.rem(y + 1, NY)
    ym = lax.rem(y + 3, NY)
    y2 = lax.rem(y + 2, NY)
    dev_xp = {"fsdp": xp * NY + y}
    dev_xm = {"fsdp": xm * NY + y}
    dev_yp = {"fsdp": x * NY + yp}
    dev_ym = {"fsdp": x * NY + ym}
    dev_c = {"tensor": 1 - c}

    def z_at(step):
        return lax.rem(z + step, NZ)

    def dev_z(step, other=0):
        if other:
            return {"dp": z_at(step), "tensor": 1 - c}
        return {"dp": z_at(step)}

    barrier = pltpu.get_barrier_semaphore()
    peers = [dev_xp, dev_xm, dev_yp, dev_ym, dev_c]
    peers += [dev_z(dz, other) for dz in range(1, NZ) for other in (0, 1)]
    for dev in peers:
        pl.semaphore_signal(barrier, inc=1, device_id=dev, device_id_type=pl.DeviceIdType.MESH)

    own = W.at[x, y, c]
    spots = [(wq, 0), (wk, 1), (wv, 2), (wo, O_AT)]
    spots += [(wg.at[:, pl.ds(i * B, B)], G_AT + i) for i in range(4)]
    spots += [(wu.at[:, pl.ds(i * B, B)], U_AT + i) for i in range(4)]
    spots += [(wd.at[pl.ds(i * B, B), :], D_AT + i) for i in range(4)]
    of_local = [0] * 3 + [1] + [2] * 4 + [3] * 4 + [4] * 4
    local = [
        pltpu.make_async_copy(ref, own.at[b], lsem.at[of_local[i]])
        for i, (ref, b) in enumerate(spots)
    ]
    for i in range(4):
        local[i].start()
    tok = [
        pltpu.make_async_copy(
            tok_hbm.at[pl.ds(i * 256, 256), :], X.at[pl.ds(i * 256, 256), :], lsem.at[5 + i]
        )
        for i in range(8)
    ]
    for i in range(8):
        tok[i].start()
    for i in range(4, 16):
        local[i].start()

    pl.semaphore_wait(barrier, len(peers))

    sent, free = [], list(range(SENDS))

    class Remote:
        def __init__(self, src, dst, rs, dev):
            self.parts = src, dst, rs, dev

        def start(self):
            src, dst, rs, dev = self.parts
            self.slot = free.pop(0)
            self.copy = pltpu.make_async_remote_copy(
                src_ref=src, dst_ref=dst, send_sem=ssem.at[self.slot], recv_sem=rs,
                device_id=dev, device_id_type=pl.DeviceIdType.MESH,
            )
            self.copy.start()
            sent.append(self)

        def wait_recv(self):
            self.copy.wait_recv()

    remote = Remote

    def go(cp):
        cp.start()

    def arrived(ref, rs):
        pltpu.make_async_copy(ref, ref, rs).wait()

    def drain(keep):
        while len(sent) > keep:
            cp = sent.pop(0)
            cp.copy.wait_send()
            free.append(cp.slot)

    def plan(g, a, b, local_at=None, kind="whole"):
        nb = pl.ds(a, b - a)
        up, dn = pl.ds(0, 64), pl.ds(64, 64)
        full = pl.ds(0, 4)
        lo, hi = pl.ds(0, 2), pl.ds(2, 2)

        def cp(s, idx, dev):
            ref = W.at[idx]
            return remote(ref, ref, wrecv.at[g * 5 + s], dev)

        sizes = ((0, lo, 0, nb), (0, 0, 0, nb), (lo, full, 0, nb), (0, full, 0, nb))

        copies = [
            ((x, y, c, nb, up), dev_xp),
            ((x, y, c, nb, up), dev_xm),
            ((x, y, c, nb, dn), dev_yp),
            ((x, y, c, nb, dn), dev_ym),
            ((xm, y, c, nb, pl.ds(0, 32)), dev_xp),
            ((xp, y, c, nb, pl.ds(32, 32)), dev_xm),
            ((x, ym, c, nb, pl.ds(64, 32)), dev_yp),
            ((x, yp, c, nb, pl.ds(96, 32)), dev_ym),
            ((full, y, c, nb, up), dev_yp),
            ((full, y, c, nb, up), dev_ym),
            ((x, full, c, nb, dn), dev_xp),
            ((x, full, c, nb, dn), dev_xm),
            ((lo, ym, c, nb, up), dev_yp),
            ((hi, yp, c, nb, up), dev_ym),
            ((xm, lo, c, nb, dn), dev_xp),
            ((xp, hi, c, nb, dn), dev_xm),
        ]
        pass_on = [
            ((x, y, c, nb),),
            ((xm, y, c, nb, up), (xp, y, c, nb, up), (x, ym, c, nb, dn), (x, yp, c, nb, dn)),
            ((x2, y, c, nb, up), (x, y2, c, nb, dn)),
            ((full, ym, c, nb, up), (full, yp, c, nb, up), (xm, full, c, nb, dn), (xp, full, c, nb, dn)),
            ((full, y2, c, nb, up), (x2, full, c, nb, dn)),
        ]
        if kind == "second":
            pass_on[2] = ((full, y, c, nb, up), (x, full, c, nb, dn))
        if kind in ("first", "alone"):
            pass_on = [()] * 5

        def stage(s):
            if s == 5:
                arrived(W.at[full, full, 1 - c, nb], wrecv.at[g * 5 + 4])
                return
            if s == 0:
                arrived(own.at[nb], lsem.at[local_at])
            elif not (kind == "second" and s == 2):
                arrived(W.at[sizes[s - 1]], wrecv.at[g * 5 + s - 1])
            if s < 4 and not (kind == "first" and s == 2):
                for i in range(4 * s, 4 * s + 4):
                    go(cp(s, *copies[i]))
            for idx in pass_on[s]:
                go(cp(4, idx, dev_c))

        return stage

    w_q = plan(0, 0, 3, 0, "alone")
    w_a = plan(1, O_AT, O_AT + 1, 1, "first")
    w_c0 = plan(2, O_AT, O_AT + 3, None, "second")
    w_c1 = plan(3, O_AT + 3, O_AT + 5, None, "second")
    w_c2 = plan(4, O_AT + 5, O_AT + 8, None, "second")
    w_g = plan(5, G_AT, U_AT, 2)
    w_u = plan(6, U_AT, D_AT, 3)
    w_d = plan(7, D_AT, BLOCKS, 4)

    def ring_o(s):
        if s > 0:
            arrived(W.at[pl.ds(0, 4), 0, 0, pl.ds(0, 2 if s < 4 else 1)], z_recv.at[s - 1])
        for part in (0, 1):
            for d in (0, 1):
                if s < 3 or (s == 3 and part == d):
                    sign = 1 if d else -1
                    here, there = O_AT + SLOT[sign * s], O_AT + SLOT[sign * (s + 1)]
                    if part == 0:
                        src = W.at[pl.ds(0, 4), y, c, here, pl.ds(0, 64)]
                        dst = W.at[pl.ds(0, 4), y, c, there, pl.ds(0, 64)]
                    else:
                        src = W.at[x, pl.ds(0, 4), c, here, pl.ds(64, 64)]
                        dst = W.at[x, pl.ds(0, 4), c, there, pl.ds(64, 64)]
                    go(remote(src, dst, z_recv.at[s], dev_z(7 if d else 1)))

    w_q(0)
    w_a(0)
    w_g(0)

    segf[pl.ds(0, 8), :] = jnp.full((8, B), -1.0, F32)
    segf[pl.ds(4, NBLK), :] = seg_ref[...].astype(F32)
    k[pl.ds(0, 512), :] = jnp.zeros((512, B), BF16)
    v[pl.ds(0, 512), :] = jnp.zeros((512, B), BF16)
    order = ord_ref[...].astype(F32)
    ordf[...] = order
    rank = lax.broadcasted_iota(jnp.int32, (NBLK, B), 0) * B + lax.broadcasted_iota(
        jnp.int32, (NBLK, B), 1
    )
    ordm[...] = jnp.where(rank < cnt_ref[j], order, -1.0)
    gain1 = jnp.concatenate([g1_ref[pl.ds(i, 1), :] for i in range(NBLK)], axis=1)
    gain2 = jnp.concatenate([g2_ref[pl.ds(i, 1), :] for i in range(NBLK)], axis=1)

    def normed(data, gain):
        f = data.astype(F32)
        inv = lax.rsqrt(jnp.mean(f * f, axis=-1, keepdims=True) + 1e-05)
        return (f * inv * gain).astype(BF16)

    def norm_chunk(i):
        tok[i].wait()

        def body(r, _):
            rows = pl.ds(pl.multiple_of(i * 256 + r * 16, 16), 16)
            XN[rows, :] = normed(X[rows, :], gain1)
            return 0

        lax.fori_loop(0, 16, body, 0, unroll=4)

    lane = lax.broadcasted_iota(jnp.int32, (B, B), 1).astype(F32)
    sub = lax.broadcasted_iota(jnp.int32, (B, B), 0).astype(F32)

    def one_hot(t, _):
        rows = pl.ds(pl.multiple_of(t * B, B), B)
        col = column_of(ordf[pl.ds(t, 1), :])
        for u in range(NBLK):
            OHP[rows, pl.ds(u * B, B)] = jnp.where(col == lane + (B * u), 1.0, 0.0).astype(BF16)
        return 0

    norm_chunk(0)
    norm_chunk(1)
    norm_chunk(2)
    w_q(1)
    w_a(1)
    w_u(0)
    norm_chunk(3)
    norm_chunk(4)
    w_q(2)
    w_a(2)
    ring_o(0)
    w_g(1)
    w_d(0)
    norm_chunk(5)
    norm_chunk(6)
    norm_chunk(7)
    lax.fori_loop(0, 10, one_hot, 0)
    w_q(3)
    ring_o(1)
    w_u(1)
    drain(24)
    w_q(4)
    w_c0(2)
    w_d(1)
    ring_o(2)
    w_c1(2)

    def blocks(cc, b, count):
        return jnp.concatenate(
            [
                jnp.concatenate([W[i // NY, i % NY, cc, b + e] for e in range(count)], axis=1)
                for i in range(16)
            ],
            axis=0,
        )

    def qkv_product(m):
        rows = pl.ds(pl.multiple_of(m * 256, 256), 256)
        return jnp.dot(XN[rows, :], blocks(c, 0, 3), preferred_element_type=F32).astype(BF16)

    def qkv_store(m, r):
        rows = pl.ds(pl.multiple_of(m * 256, 256), 256)
        q[rows, :] = r[:, 0:B]
        rows = pl.ds(pl.multiple_of(512 + m * 256, 256), 256)
        k[rows, :] = r[:, B : 2 * B]
        v[rows, :] = r[:, 2 * B : 3 * B]

    scale = math.log2(math.e) / math.sqrt(B)
    below = lax.broadcasted_iota(jnp.int32, (256, 256), 1) <= lax.broadcasted_iota(
        jnp.int32, (256, 256), 0
    )

    def attend(i):
        qrows = pl.ds(pl.multiple_of(i * 256, 256), 256)
        krows = pl.ds(pl.multiple_of(i * 256, 256), 768)
        s = lax.dot_general(
            q[qrows, :], k[krows, :], (((1,), (1,)), ((), ())), preferred_element_type=F32
        )
        segq = jnp.concatenate(
            [column_of(segf[pl.ds(2 * i + 4 + e, 1), :]) for e in range(2)], axis=0
        )
        parts = [
            jnp.where(segq == segf[pl.ds(2 * i + t, 1), :], s[:, t * B : (t + 1) * B], -1e30)
            for t in range(6)
        ]
        s = jnp.concatenate(
            parts[:4]
            + [jnp.where(below[:, e * B : (e + 1) * B], parts[4 + e], -1e30) for e in range(2)],
            axis=1,
        )
        e = jnp.exp2((s - jnp.max(s, axis=-1, keepdims=True)) * scale)
        p = (e * (1.0 / jnp.sum(e, axis=-1, keepdims=True))).astype(BF16)
        return jnp.dot(p, v[krows, :], preferred_element_type=F32).astype(BF16)

    def att_store(i, value):
        att[pl.ds(pl.multiple_of(i * 256, 256), 256), :] = value

    def both(m, _):
        done = attend(m - 1)
        r = qkv_product(m)
        att_store(m - 1, done)
        qkv_store(m, r)
        return 0

    qkv_store(0, qkv_product(0))
    lax.fori_loop(1, 3, both, 0)
    ring_o(3)
    w_c0(3)
    lax.fori_loop(3, 5, both, 0)
    ring_o(4)
    w_c2(2)
    w_c1(3)
    lax.fori_loop(5, 8, both, 0)
    att_store(7, attend(7))
    w_c0(4)
    drain(32)

    def pick(cc):
        def tile(t, _):
            rows = pl.ds(pl.multiple_of(cc * HALF + t * QTR, 64), QTR)
            PICK[rows, :] = jnp.dot(
                OHP[rows, :], att[...], preferred_element_type=F32
            ).astype(BF16)
            return 0

        lax.fori_loop(0, 2, tile, 0)

    def piece_rows(zs, cc):
        return pl.ds(pl.multiple_of(cc * HALF + zs * PIECE, 16), PIECE)

    for other in (1, 0):
        cc = 1 - c if other else c
        pick(cc)
        for dz in (4, 3, 5, 2, 6, 1, 7, 0):
            if dz == 0 and other == 0:
                continue
            dev = dev_z(dz, other) if dz else dev_c
            go(remote(PICK.at[piece_rows(z_at(dz), cc)], A2.at[2 * z + c], z_recv.at[4], dev))
    A2[2 * z + c] = PICK[piece_rows(z, c), :]

    w_c2(3)
    w_c1(4)
    w_g(2)
    w_u(2)

    def row_tokens(n, _):
        cols = pl.ds(pl.multiple_of(n * 256, 256), 256)
        AGB[z, :, cols] = jnp.dot(
            OHP[piece_rows(z, c), :], X[:, cols], preferred_element_type=F32
        ).astype(BF16)
        return 0

    lax.fori_loop(0, 8, row_tokens, 0)
    w_c2(4)
    drain(40)

    def put_hot(t, _):
        rows = pl.ds(pl.multiple_of(t * B, B), B)
        base = (t * B).astype(F32)
        for u in range(10):
            XN[rows, pl.ds(u * B, B)] = jnp.where(
                ordm[pl.ds(u, 1), :] == sub + base, 1.0, 0.0
            ).astype(BF16)
        return 0

    ones = jnp.ones((2 * HALF, B), BF16)

    def live(t, _):
        rows = pl.ds(pl.multiple_of(t * 256, 256), 256)
        LIVE[rows, :] = jnp.dot(
            XN[rows, pl.ds(0, 2 * HALF)], ones, preferred_element_type=F32
        ).astype(BF16)
        return 0

    arrived(A2.at[pl.ds(0, 15)], z_recv.at[4])
    w_c0(5)
    w_c1(5)
    w_c2(5)

    def w_index(n):
        return n // 2, 2 * lax.rem(n, 2)

    def ring_copy(base, src, dst, d, s, h):
        n = base + (d * 4 + s) * 2 + h
        return remote(src, dst, z_recv.at[n], dev_z(1) if d == 0 else dev_z(7))

    ag = {}

    def ag_copy(d, s, h):
        if (d, s, h) not in ag:
            src = z_at(NZ - s) if d == 0 else z_at(s)
            ref = AGB.at[src, :, pl.ds(h * 1024, 1024)]
            ag[d, s, h] = ring_copy(8, ref, ref, d, s, h)
        return ag[d, s, h]

    def out_proj(n, _):
        xw, yw = w_index(n)
        cols = pl.ds(pl.multiple_of(n * 256, 256), 256)
        rhs = jnp.concatenate(
            [
                jnp.concatenate([W[xw, yw + e, cc, O_AT + slot] for e in range(2)], axis=1)
                for slot in range(8)
                for cc in range(2)
            ],
            axis=0,
        )
        lhs = jnp.concatenate(
            [A2[2 * z_at(STEP_OF_SLOT[slot]) + cc] for slot in range(8) for cc in range(2)], axis=1
        )
        total = jnp.dot(lhs, rhs, preferred_element_type=F32)
        AGB[z, :, cols] = (AGB[z, :, cols].astype(F32) + total).astype(BF16)
        return 0

    for h in (0, 1):
        lax.fori_loop(4 * h, 4 * h + 4, out_proj, 0)
        for d in (0, 1):
            go(ag_copy(d, 0, h))

    batches = ([z, z_at(1), z_at(7), z_at(2)], [z_at(6), z_at(3), z_at(5)], [z_at(4)])

    def prepare(at):
        zs = sum(batches, [])[at]
        for r in range(0, PIECE, 16):
            NRM[pl.ds(at * PIECE + r, 16), :] = normed(AGB[zs, pl.ds(r, 16), :], gain2)

    def ff_in(batch, begin=0, end=4):
        def body(n, _):
            cc = n // 2
            e = 2 * lax.rem(n, 2)
            lhs = NRM[pl.ds((0, 4, 7)[batch] * PIECE, len(batches[batch]) * PIECE), :]
            g = jnp.dot(lhs, blocks(cc, G_AT + e, 2), preferred_element_type=F32)
            u = jnp.dot(lhs, blocks(cc, U_AT + e, 2), preferred_element_type=F32)
            hid = (g / (1.0 + jnp.exp(-g)) * u).astype(BF16)
            cols = pl.ds(pl.multiple_of(n * 256, 256), 256)
            for i, zs in enumerate(batches[batch]):
                H[pl.ds(pl.multiple_of(zs * PIECE, 16), PIECE), cols] = hid[
                    i * PIECE : (i + 1) * PIECE
                ]
            return 0

        lax.fori_loop(begin, end, body, 0)

    def receive(s, h):
        for d in (0, 1):
            if s == 3 and h != d:
                continue
            ag_copy(d, s, h).wait_recv()
            if s < 2 or (s == 2 and h == d):
                go(ag_copy(d, s + 1, h))

    prepare(0)
    lax.fori_loop(0, 16, put_hot, 0)
    w_g(3)
    w_d(2)
    lax.fori_loop(0, 8, live, 0)
    receive(0, 0)
    drain(40)
    receive(0, 1)
    w_u(3)
    prepare(1)
    prepare(2)
    drain(40)
    receive(1, 0)
    w_g(4)
    receive(1, 1)
    w_d(3)
    prepare(3)
    prepare(4)
    drain(40)
    receive(2, 0)
    w_u(4)
    w_g(5)
    w_u(5)
    ff_in(0, 0, 2)
    receive(2, 1)
    w_d(4)
    ff_in(0, 2, 4)
    prepare(5)
    prepare(6)
    ff_in(1)
    receive(3, 0)
    receive(3, 1)
    prepare(7)
    ff_in(2)
    w_d(5)

    def rows_of(h):
        return pl.ds(h * QTR, QTR)

    def partial(zd, h):
        xw, yw = w_index(zd)
        rhs = jnp.concatenate(
            [
                jnp.concatenate([W[xw, yw + e, cc, D_AT + b] for e in range(2)], axis=1)
                for cc in range(2)
                for b in range(4)
            ],
            axis=0,
        )
        return jnp.dot(H[rows_of(h), :], rhs, preferred_element_type=F32)

    copies = {}
    for d in (0, 1):
        RB2[d] = partial(z_at(4), d).astype(BF16)
        copies[d, 0, d] = ring_copy(24, RB2.at[d], RS2.at[d, 0, d], d, 0, d)
        go(copies[d, 0, d])
    for s in (1, 2, 3):
        for d, h in ((0, 1), (1, 0), (0, 0), (1, 1)):
            part = partial(z_at(4 - s) if d == 0 else z_at(4 + s), h)
            slot = RS2.at[d, s - 1, h]
            if (d, s - 1, h) in copies:
                copies[d, s - 1, h].wait_recv()
                part = part + slot[...].astype(F32)
            slot[...] = part.astype(BF16)
            copies[d, s, h] = ring_copy(24, slot, RS2.at[d, s, h], d, s, h)
            go(copies[d, s, h])
        drain(16)
    mine = pl.ds(pl.multiple_of(z * 256, 256), 256)
    for h in (1, 0):
        total = partial(z, h)
        copies[0, 3, h].wait_recv()
        copies[1, 3, h].wait_recv()
        total = total + RS2[0, 3, h].astype(F32) + RS2[1, 3, h].astype(F32)
        carried = jnp.concatenate([AGB[4 * h + i, :, mine] for i in range(4)], axis=0)
        fin = (carried.astype(F32) + total).astype(BF16)
        FIN[c, rows_of(h), :] = jnp.where(c == 0, fin[:, :B], fin[:, B:])
        FSND[rows_of(h), :] = jnp.where(c == 0, fin[:, B:], fin[:, :B])
    swap = remote(FSND, FIN.at[c], z_recv.at[5], dev_c)
    go(swap)

    def put_own(t, _):
        rows = pl.ds(pl.multiple_of(t * 256, 256), 256)
        P1[rows, :] = jnp.dot(
            XN[rows, pl.ds(pl.multiple_of(c * HALF, B), HALF)], FIN[c], preferred_element_type=F32
        ).astype(BF16)
        return 0

    lax.fori_loop(0, 8, put_own, 0)
    swap.wait_recv()
    cols = pl.ds(pl.multiple_of((2 * z + c) * B, B), B)

    def put(t, _):
        rows = pl.ds(pl.multiple_of(t * 256, 256), 256)
        part = jnp.dot(
            XN[rows, pl.ds(pl.multiple_of((1 - c) * HALF, B), HALF)], FIN[1 - c],
            preferred_element_type=F32,
        )
        value = part + P1[rows, :].astype(F32)
        old = X[rows, cols].astype(F32)
        OUT[rows, :] = jnp.where(LIVE[rows, :].astype(F32) > 0.5, value, old).astype(BF16)
        store(t).start()
        return 0

    def store(t):
        rows = pl.ds(pl.multiple_of(t * 256, 256), 256)
        return pltpu.make_async_copy(OUT.at[rows, :], out_ref.at[rows, :], lsem.at[5 + t])

    lax.fori_loop(0, 8, put, 0)
    for t in range(8):
        store(t).wait()
    drain(0)


def body(
    tokens, segment_ids, row_order, row_counts, first_gain, second_gain,
    query_weight, key_weight, value_weight, output_weight, gate_weight, up_weight, down_weight,
):
    vm = pl.BlockSpec(memory_space=pltpu.VMEM)
    anyspace = pl.BlockSpec(memory_space=pl.ANY)
    smem = pl.BlockSpec(memory_space=pltpu.SMEM)
    return pl.pallas_call(
        kernel,
        out_shape=jax.ShapeDtypeStruct((ROWS, B), BF16),
        in_specs=[anyspace, vm, vm, smem, vm, vm] + [anyspace] * 7,
        out_specs=anyspace,
        scratch_shapes=[
            pltpu.VMEM((NX, NY, 2, BLOCKS, B, B), BF16),
            pltpu.VMEM((ROWS, D), BF16),
            pltpu.VMEM((ROWS, D), BF16),
            pltpu.VMEM((ROWS, B), BF16),
            pltpu.VMEM((ROWS + 512, B), BF16),
            pltpu.VMEM((ROWS + 512, B), BF16),
            pltpu.VMEM((ROWS, B), BF16),
            pltpu.VMEM((2 * HALF, ROWS), BF16),
            pltpu.VMEM((2 * HALF, B), BF16),
            pltpu.VMEM((16, PIECE, B), BF16),
            pltpu.VMEM((NZ, PIECE, D), BF16),
            pltpu.VMEM((HALF, D), BF16),
            pltpu.VMEM((HALF, 1024), BF16),
            pltpu.VMEM((2, 4, 2, QTR, 2 * B), BF16),
            pltpu.VMEM((2, QTR, 2 * B), BF16),
            pltpu.VMEM((2, HALF, B), BF16),
            pltpu.VMEM((HALF, B), BF16),
            pltpu.VMEM((ROWS, B), BF16),
            pltpu.VMEM((ROWS, B), BF16),
            pltpu.VMEM((ROWS, B), BF16),
            pltpu.VMEM((24, B), F32),
            pltpu.VMEM((NBLK, B), F32),
            pltpu.VMEM((NBLK, B), F32),
            pltpu.SemaphoreType.DMA((13,)),
            pltpu.SemaphoreType.DMA((SENDS,)),
            pltpu.SemaphoreType.DMA((8 * 5,)),
            pltpu.SemaphoreType.DMA((40,)),
        ],
        compiler_params=pltpu.CompilerParams(
            collective_id=0, has_side_effects=True, vmem_limit_bytes=67 * 1000 * 1000
        ),
        name="recursion_step",
    )(
        tokens,
        segment_ids.reshape(NBLK, B),
        row_order.reshape(NBLK, B),
        row_counts,
        first_gain.reshape(NBLK, B),
        second_gain.reshape(NBLK, B),
        query_weight, key_weight, value_weight, output_weight,
        gate_weight, up_weight, down_weight,
    )


def solution(mesh):
    weight = P("fsdp", ("dp", "tensor"))
    weight_t = P(("dp", "tensor"), "fsdp")
    in_specs = (
        P("fsdp", None), P("fsdp"), P("fsdp"), P(), P(), P(),
        weight, weight, weight, weight_t, weight, weight, weight_t,
    )
    return jax.shard_map(
        body, mesh=mesh, in_specs=in_specs, out_specs=weight, check_vma=False
    )
```

```python
import math

import jax
import jax.numpy as jnp
from jax import lax
from jax.experimental import pallas as pl
from jax.experimental.pallas import tpu as pltpu
from jax.sharding import PartitionSpec as P

F32 = jnp.float32
BF16 = jnp.bfloat16
NZ = 8
NX = 4
NY = 4
B = 128
ROWS = 2048
D = 2048
HALF = 640
QTR = 320
NBLK = 16
PIECE = 80
O_AT, G_AT, U_AT, D_AT, BLOCKS = 3, 11, 15, 19, 23
SENDS = 96
SLOT = {0: 0, 1: 1, -1: 2, 2: 3, -2: 4, 3: 5, -3: 6, 4: 7, -4: 7}
STEP_OF_SLOT = (0, 1, 7, 2, 6, 3, 5, 4)


def column_of(row):
    return jnp.transpose(jnp.broadcast_to(row, (B, B)))


def kernel(
    tok_hbm, seg_hbm, ord_hbm, cnt_ref, g1_hbm, g2_hbm,
    wq, wk, wv, wo, wg, wu, wd,
    out_ref,
    W, X, XN, q, k, v, att, OHP, PICK, A2, AGB, NRM, H, RS2, RB2, FIN, FSND, P1, LIVE, OUT,
    segf, ordf, ordm, seg_ref, ord_ref, g1_ref, g2_ref,
    lsem, ssem, wrecv, z_recv,
):
    z = lax.axis_index("dp")
    j = lax.axis_index("fsdp")
    c = lax.axis_index("tensor")
    x = j // NY
    y = lax.rem(j, NY)
    xp = lax.rem(x + 1, NX)
    xm = lax.rem(x + 3, NX)
    x2 = lax.rem(x + 2, NX)
    yp = lax.rem(y + 1, NY)
    ym = lax.rem(y + 3, NY)
    y2 = lax.rem(y + 2, NY)
    dev_xp = {"fsdp": xp * NY + y}
    dev_xm = {"fsdp": xm * NY + y}
    dev_yp = {"fsdp": x * NY + yp}
    dev_ym = {"fsdp": x * NY + ym}
    dev_c = {"tensor": 1 - c}

    def z_at(step):
        return lax.rem(z + step, NZ)

    def dev_z(step, other=0):
        if other:
            return {"dp": z_at(step), "tensor": 1 - c}
        return {"dp": z_at(step)}

    barrier = pltpu.get_barrier_semaphore()
    peers = [dev_xp, dev_xm, dev_yp, dev_ym, dev_c]
    peers += [dev_z(dz, other) for dz in range(1, NZ) for other in (0, 1)]
    for dev in peers:
        pl.semaphore_signal(barrier, inc=1, device_id=dev, device_id_type=pl.DeviceIdType.MESH)

    own = W.at[x, y, c]
    spots = [(wq, 0), (wk, 1), (wv, 2), (wo, O_AT)]
    spots += [(wg.at[:, pl.ds(i * B, B)], G_AT + i) for i in range(4)]
    spots += [(wu.at[:, pl.ds(i * B, B)], U_AT + i) for i in range(4)]
    spots += [(wd.at[pl.ds(i * B, B), :], D_AT + i) for i in range(4)]
    of_local = [0] * 3 + [1] + [2] * 4 + [3] * 4 + [4] * 4
    local = [
        pltpu.make_async_copy(ref, own.at[b], lsem.at[of_local[i]])
        for i, (ref, b) in enumerate(spots)
    ]
    for i in range(4):
        local[i].start()
    tok = [
        pltpu.make_async_copy(
            tok_hbm.at[pl.ds(i * 256, 256), :], X.at[pl.ds(i * 256, 256), :], lsem.at[5 + i]
        )
        for i in range(8)
    ]
    small = [
        pltpu.make_async_copy(src, dst, lsem.at[13 + i])
        for i, (src, dst) in enumerate(
            ((seg_hbm, seg_ref), (ord_hbm, ord_ref), (g1_hbm, g1_ref), (g2_hbm, g2_ref))
        )
    ]
    for cp in small:
        cp.start()
    for i in range(8):
        tok[i].start()
    for i in range(4, 16):
        local[i].start()

    pl.semaphore_wait(barrier, len(peers))

    sent, free = [], list(range(SENDS))

    class Remote:
        def __init__(self, src, dst, rs, dev):
            self.parts = src, dst, rs, dev

        def make(self):
            src, dst, rs, dev = self.parts
            self.slot = free.pop(0)
            self.copy = pltpu.make_async_remote_copy(
                src_ref=src, dst_ref=dst, send_sem=ssem.at[self.slot], recv_sem=rs,
                device_id=dev, device_id_type=pl.DeviceIdType.MESH,
            )
            sent.append(self)

        def start(self):
            self.make()
            self.copy.start()

        def wait_recv(self):
            self.copy.wait_recv()

    remote = Remote

    def go(cp):
        cp.start()

    def go_on_even(cp):
        cp.make()

        @pl.when(c == 0)
        def _():
            cp.copy.start()

        return cp.copy

    def arrived(ref, rs):
        pltpu.make_async_copy(ref, ref, rs).wait()

    def drain(keep):
        while len(sent) > keep:
            cp = sent.pop(0)
            cp.copy.wait_send()
            free.append(cp.slot)

    used = []

    def recv_sem(g, s):
        if (g, s) not in used:
            used.append((g, s))
        return wrecv.at[used.index((g, s))]

    def plan(g, a, b, local_at=None, kind="whole"):
        nb = pl.ds(a, b - a)
        up, dn = pl.ds(0, 64), pl.ds(64, 64)
        full = pl.ds(0, 4)
        lo, hi = pl.ds(0, 2), pl.ds(2, 2)

        def cp(s, idx, dev):
            ref = W.at[idx]
            return remote(ref, ref, recv_sem(g, s), dev)

        sizes = ((0, lo, 0, nb), (0, 0, 0, nb), (lo, full, 0, nb), (0, full, 0, nb))

        copies = [
            ((x, y, c, nb, up), dev_xp),
            ((x, y, c, nb, up), dev_xm),
            ((x, y, c, nb, dn), dev_yp),
            ((x, y, c, nb, dn), dev_ym),
            ((xm, y, c, nb, pl.ds(0, 32)), dev_xp),
            ((xp, y, c, nb, pl.ds(32, 32)), dev_xm),
            ((x, ym, c, nb, pl.ds(64, 32)), dev_yp),
            ((x, yp, c, nb, pl.ds(96, 32)), dev_ym),
            ((full, y, c, nb, up), dev_yp),
            ((full, y, c, nb, up), dev_ym),
            ((x, full, c, nb, dn), dev_xp),
            ((x, full, c, nb, dn), dev_xm),
            ((lo, ym, c, nb, up), dev_yp),
            ((hi, yp, c, nb, up), dev_ym),
            ((xm, lo, c, nb, dn), dev_xp),
            ((xp, hi, c, nb, dn), dev_xm),
        ]
        pass_on = [
            ((x, y, c, nb),),
            ((xm, y, c, nb, up), (xp, y, c, nb, up), (x, ym, c, nb, dn), (x, yp, c, nb, dn)),
            ((x2, y, c, nb, up), (x, y2, c, nb, dn)),
            ((full, ym, c, nb, up), (full, yp, c, nb, up), (xm, full, c, nb, dn), (xp, full, c, nb, dn)),
            ((full, y2, c, nb, up), (x2, full, c, nb, dn)),
        ]
        if kind == "second":
            pass_on[2] = ((full, y, c, nb, up), (x, full, c, nb, dn))
        if kind in ("first", "alone"):
            pass_on = [()] * 5

        held = []

        def stage(s, core=None):
            if core == 1:
                @pl.when(c == 1)
                def _():
                    for h in held:
                        h.start()
                return
            if s == 5:
                arrived(W.at[full, full, 1 - c, nb], recv_sem(g, 4))
                return
            if s == 0:
                arrived(own.at[nb], lsem.at[local_at])
            elif not (kind == "second" and s == 2):
                arrived(W.at[sizes[s - 1]], recv_sem(g, s - 1))
            if s < 4 and not (kind == "first" and s == 2):
                for i in range(4 * s, 4 * s + 4):
                    if core == 0:
                        held.append(go_on_even(cp(s, *copies[i])))
                    else:
                        go(cp(s, *copies[i]))
            for idx in pass_on[s]:
                go(cp(4, idx, dev_c))

        return stage

    w_q = plan(0, 0, 3, 0, "alone")
    w_a = plan(1, O_AT, O_AT + 1, 1, "first")
    w_c0 = plan(2, O_AT, O_AT + 3, None, "second")
    w_c1 = plan(3, O_AT + 3, O_AT + 5, None, "second")
    w_c2 = plan(4, O_AT + 5, O_AT + 8, None, "second")
    w_g = plan(5, G_AT, U_AT, 2)
    w_u = plan(6, U_AT, D_AT, 3)
    w_d = plan(7, D_AT, BLOCKS, 4)

    def ring_o(s):
        if s > 0:
            arrived(W.at[pl.ds(0, 4), 0, 0, pl.ds(0, 2 if s < 4 else 1)], z_recv.at[s - 1])
        for part in (0, 1):
            for d in (0, 1):
                if s < 3 or (s == 3 and part == d):
                    sign = 1 if d else -1
                    here, there = O_AT + SLOT[sign * s], O_AT + SLOT[sign * (s + 1)]
                    if part == 0:
                        src = W.at[pl.ds(0, 4), y, c, here, pl.ds(0, 64)]
                        dst = W.at[pl.ds(0, 4), y, c, there, pl.ds(0, 64)]
                    else:
                        src = W.at[x, pl.ds(0, 4), c, here, pl.ds(64, 64)]
                        dst = W.at[x, pl.ds(0, 4), c, there, pl.ds(64, 64)]
                    go(remote(src, dst, z_recv.at[s], dev_z(7 if d else 1)))

    w_q(0)
    w_a(0)
    w_g(0)

    for cp in small:
        cp.wait()
    segf[pl.ds(0, 8), :] = jnp.full((8, B), -1.0, F32)
    segf[pl.ds(4, NBLK), :] = seg_ref[...].astype(F32)
    k[pl.ds(0, 512), :] = jnp.zeros((512, B), BF16)
    v[pl.ds(0, 512), :] = jnp.zeros((512, B), BF16)
    order = ord_ref[...].astype(F32)
    ordf[...] = order
    rank = lax.broadcasted_iota(jnp.int32, (NBLK, B), 0) * B + lax.broadcasted_iota(
        jnp.int32, (NBLK, B), 1
    )
    ordm[...] = jnp.where(rank < cnt_ref[j], order, -1.0)
    gain1 = jnp.concatenate([g1_ref[pl.ds(i, 1), :] for i in range(NBLK)], axis=1)
    gain2 = jnp.concatenate([g2_ref[pl.ds(i, 1), :] for i in range(NBLK)], axis=1)

    def normed(data, gain):
        f = data.astype(F32)
        inv = lax.rsqrt(jnp.mean(f * f, axis=-1, keepdims=True) + 1e-05)
        return (f * inv * gain).astype(BF16)

    def norm_chunk(i):
        tok[i].wait()

        def body(r, _):
            rows = pl.ds(pl.multiple_of(i * 256 + r * 16, 16), 16)
            XN[rows, :] = normed(X[rows, :], gain1)
            return 0

        lax.fori_loop(0, 16, body, 0, unroll=4)

    lane = lax.broadcasted_iota(jnp.int32, (B, B), 1).astype(F32)
    sub = lax.broadcasted_iota(jnp.int32, (B, B), 0).astype(F32)

    def one_hot(t, _):
        rows = pl.ds(pl.multiple_of(t * B, B), B)
        col = column_of(ordf[pl.ds(t, 1), :])
        for u in range(NBLK):
            OHP[rows, pl.ds(u * B, B)] = jnp.where(col == lane + (B * u), 1.0, 0.0).astype(BF16)
        return 0

    norm_chunk(0)
    norm_chunk(1)
    norm_chunk(2)
    w_q(1)
    w_a(1)
    w_u(0)
    norm_chunk(3)
    norm_chunk(4)
    w_q(2)
    w_a(2)
    ring_o(0)
    w_g(1)
    w_d(0)
    norm_chunk(5)
    norm_chunk(6)
    norm_chunk(7)
    lax.fori_loop(0, 10, one_hot, 0)
    ring_o(1)
    w_q(3)
    w_u(1)
    drain(24)
    ring_o(2)
    w_q(4)
    w_c0(2)
    w_d(1)
    w_c1(2)

    def blocks(cc, b, count):
        return jnp.concatenate(
            [
                jnp.concatenate([W[i // NY, i % NY, cc, b + e] for e in range(count)], axis=1)
                for i in range(16)
            ],
            axis=0,
        )

    def qkv_product(m):
        rows = pl.ds(pl.multiple_of(m * 256, 256), 256)
        return jnp.dot(XN[rows, :], blocks(c, 0, 3), preferred_element_type=F32).astype(BF16)

    def qkv_store(m, r):
        rows = pl.ds(pl.multiple_of(m * 256, 256), 256)
        q[rows, :] = r[:, 0:B]
        rows = pl.ds(pl.multiple_of(512 + m * 256, 256), 256)
        k[rows, :] = r[:, B : 2 * B]
        v[rows, :] = r[:, 2 * B : 3 * B]

    scale = math.log2(math.e) / math.sqrt(B)
    below = lax.broadcasted_iota(jnp.int32, (256, 256), 1) <= lax.broadcasted_iota(
        jnp.int32, (256, 256), 0
    )

    def scores(i):
        qrows = pl.ds(pl.multiple_of(i * 256, 256), 256)
        krows = pl.ds(pl.multiple_of(i * 256, 256), 768)
        return lax.dot_general(
            q[qrows, :], k[krows, :], (((1,), (1,)), ((), ())), preferred_element_type=F32
        )

    def attend(i, s):
        krows = pl.ds(pl.multiple_of(i * 256, 256), 768)
        segq = jnp.concatenate(
            [column_of(segf[pl.ds(2 * i + 4 + e, 1), :]) for e in range(2)], axis=0
        )
        parts = [
            jnp.where(segq == segf[pl.ds(2 * i + t, 1), :], s[:, t * B : (t + 1) * B], -1e30)
            for t in range(6)
        ]
        s = jnp.concatenate(
            parts[:4]
            + [jnp.where(below[:, e * B : (e + 1) * B], parts[4 + e], -1e30) for e in range(2)],
            axis=1,
        )
        e = jnp.exp2((s - jnp.max(s, axis=-1, keepdims=True)) * scale)
        p = (e * (1.0 / jnp.sum(e, axis=-1, keepdims=True))).astype(BF16)
        return jnp.dot(p, v[krows, :], preferred_element_type=F32).astype(BF16)

    def att_store(i, value):
        att[pl.ds(pl.multiple_of(i * 256, 256), 256), :] = value

    def both(m, _):
        raw = scores(m - 1)
        r = qkv_product(m)
        done = attend(m - 1, raw)
        att_store(m - 1, done)
        qkv_store(m, r)
        return 0

    qkv_store(0, qkv_product(0))
    lax.fori_loop(1, 4, both, 0)
    ring_o(3)
    lax.fori_loop(4, 7, both, 0)
    w_c0(3)
    ring_o(4)
    w_c2(2)
    w_c1(3)
    lax.fori_loop(7, 8, both, 0)
    att_store(7, attend(7, scores(7)))
    drain(32)

    def pick(cc):
        def tile(t, _):
            rows = pl.ds(pl.multiple_of(cc * HALF + t * QTR, 64), QTR)
            PICK[rows, :] = jnp.dot(
                OHP[rows, :], att[...], preferred_element_type=F32
            ).astype(BF16)
            return 0

        lax.fori_loop(0, 2, tile, 0)

    def piece_rows(zs, cc):
        return pl.ds(pl.multiple_of(cc * HALF + zs * PIECE, 16), PIECE)

    for other in (1, 0):
        cc = 1 - c if other else c
        pick(cc)
        for dz in (4, 3, 5, 2, 6, 1, 7, 0):
            if dz == 0 and other == 0:
                continue
            dev = dev_z(dz, other) if dz else dev_c
            go(remote(PICK.at[piece_rows(z_at(dz), cc)], A2.at[2 * z + c], z_recv.at[4], dev))
    A2[2 * z + c] = PICK[piece_rows(z, c), :]

    w_c2(3)
    w_c0(4)
    w_c1(4)
    w_g(2, 0)
    w_u(2, 0)

    def row_tokens(n, _):
        cols = pl.ds(pl.multiple_of(n * 256, 256), 256)
        AGB[z, :, cols] = jnp.dot(
            OHP[piece_rows(z, c), :], X[:, cols], preferred_element_type=F32
        ).astype(BF16)
        return 0

    lax.fori_loop(0, 8, row_tokens, 0)
    w_c2(4)

    def put_hot(t, _):
        rows = pl.ds(pl.multiple_of(t * B, B), B)
        base = (t * B).astype(F32)
        for u in range(10):
            XN[rows, pl.ds(u * B, B)] = jnp.where(
                ordm[pl.ds(u, 1), :] == sub + base, 1.0, 0.0
            ).astype(BF16)
        return 0

    ones = jnp.ones((2 * HALF, B), BF16)

    def live(t, _):
        rows = pl.ds(pl.multiple_of(t * 256, 256), 256)
        LIVE[rows, :] = jnp.dot(
            XN[rows, pl.ds(0, 2 * HALF)], ones, preferred_element_type=F32
        ).astype(BF16)
        return 0

    arrived(A2.at[pl.ds(0, 15)], z_recv.at[4])
    w_g(2, 1)
    w_u(2, 1)
    w_c0(5)
    w_c1(5)
    w_c2(5)

    def w_index(n):
        return n // 2, 2 * lax.rem(n, 2)

    def ring_copy(base, src, dst, d, s, h):
        n = base + d * 7 + ((0 if s == 0 else 2 * s - 1 + h) if base == 20 else (6 if s == 3 else 2 * s + h))
        return remote(src, dst, z_recv.at[n], dev_z(1) if d == 0 else dev_z(7))

    ag = {}

    def ag_copy(d, s, h):
        if (d, s, h) not in ag:
            src = z_at(NZ - s) if d == 0 else z_at(s)
            ref = AGB.at[src, :, pl.ds(h * 1024, 1024)]
            ag[d, s, h] = ring_copy(6, ref, ref, d, s, h)
        return ag[d, s, h]

    def out_proj(n, _):
        xw, yw = w_index(n)
        cols = pl.ds(pl.multiple_of(n * 256, 256), 256)
        rhs = jnp.concatenate(
            [
                jnp.concatenate([W[xw, yw + e, cc, O_AT + slot] for e in range(2)], axis=1)
                for slot in range(8)
                for cc in range(2)
            ],
            axis=0,
        )
        lhs = jnp.concatenate(
            [A2[2 * z_at(STEP_OF_SLOT[slot]) + cc] for slot in range(8) for cc in range(2)], axis=1
        )
        total = jnp.dot(lhs, rhs, preferred_element_type=F32)
        AGB[z, :, cols] = (AGB[z, :, cols].astype(F32) + total).astype(BF16)
        return 0

    for h in (0, 1):
        lax.fori_loop(4 * h, 4 * h + 4, out_proj, 0)
        for d in (0, 1):
            go(ag_copy(d, 0, h))

    batches = ([z, z_at(1), z_at(7), z_at(2)], [z_at(6), z_at(3), z_at(5)], [z_at(4)])

    def prepare(at):
        zs = sum(batches, [])[at]
        for r in range(0, PIECE, 16):
            NRM[pl.ds(at * PIECE + r, 16), :] = normed(AGB[zs, pl.ds(r, 16), :], gain2)

    def ff_in(batch, begin=0, end=4):
        def body(n, _):
            cc = n // 2
            e = 2 * lax.rem(n, 2)
            lhs = NRM[pl.ds((0, 4, 7)[batch] * PIECE, len(batches[batch]) * PIECE), :]
            g = jnp.dot(lhs, blocks(cc, G_AT + e, 2), preferred_element_type=F32)
            u = jnp.dot(lhs, blocks(cc, U_AT + e, 2), preferred_element_type=F32)
            hid = (g / (1.0 + jnp.exp(-g)) * u).astype(BF16)
            cols = pl.ds(pl.multiple_of(n * 256, 256), 256)
            for i, zs in enumerate(batches[batch]):
                H[pl.ds(pl.multiple_of(zs * PIECE, 16), PIECE), cols] = hid[
                    i * PIECE : (i + 1) * PIECE
                ]
            return 0

        lax.fori_loop(begin, end, body, 0)

    def receive(s, h):
        for d in (0, 1):
            if s == 3 and h != d:
                continue
            ag_copy(d, s, h).wait_recv()
            if s < 2 or (s == 2 and h == d):
                go(ag_copy(d, s + 1, h))

    prepare(0)
    lax.fori_loop(0, 16, put_hot, 0)
    w_g(3)
    lax.fori_loop(0, 8, live, 0)
    receive(0, 0)
    drain(40)
    w_u(3)
    w_d(2)
    receive(0, 1)
    prepare(1)
    prepare(2)
    drain(40)
    receive(1, 0)
    w_g(4)
    receive(1, 1)
    prepare(3)
    prepare(4)
    w_u(4)
    receive(2, 0)
    w_g(5)
    w_u(5)
    ff_in(0, 0, 2)
    receive(2, 1)
    w_d(3)
    ff_in(0, 2, 4)
    drain(40)
    prepare(5)
    prepare(6)
    ff_in(1)
    w_d(4)
    receive(3, 0)
    receive(3, 1)
    prepare(7)
    ff_in(2)
    w_d(5)

    def rows_of(h):
        return pl.ds(h * QTR, QTR)

    def partial(zd, h):
        xw, yw = w_index(zd)
        rhs = jnp.concatenate(
            [
                jnp.concatenate([W[xw, yw + e, cc, D_AT + b] for e in range(2)], axis=1)
                for cc in range(2)
                for b in range(4)
            ],
            axis=0,
        )
        return jnp.dot(H[rows_of(h), :], rhs, preferred_element_type=F32)

    copies = {}
    for d in (0, 1):
        RB2[d] = partial(z_at(4), d).astype(BF16)
        copies[d, 0, d] = ring_copy(20, RB2.at[d], RS2.at[d, 0, d], d, 0, d)
        go(copies[d, 0, d])
    for s in (1, 2, 3):
        for d, h in ((0, 1), (1, 0), (0, 0), (1, 1)):
            part = partial(z_at(4 - s) if d == 0 else z_at(4 + s), h)
            slot = RS2.at[d, s - 1, h]
            if (d, s - 1, h) in copies:
                copies[d, s - 1, h].wait_recv()
                part = part + slot[...].astype(F32)
            slot[...] = part.astype(BF16)
            copies[d, s, h] = ring_copy(20, slot, RS2.at[d, s, h], d, s, h)
            go(copies[d, s, h])
        drain(16)
    mine = pl.ds(pl.multiple_of(z * 256, 256), 256)
    for h in (1, 0):
        total = partial(z, h)
        copies[0, 3, h].wait_recv()
        copies[1, 3, h].wait_recv()
        total = total + RS2[0, 3, h].astype(F32) + RS2[1, 3, h].astype(F32)
        carried = jnp.concatenate([AGB[4 * h + i, :, mine] for i in range(4)], axis=0)
        fin = (carried.astype(F32) + total).astype(BF16)
        FIN[c, rows_of(h), :] = jnp.where(c == 0, fin[:, :B], fin[:, B:])
        FSND[rows_of(h), :] = jnp.where(c == 0, fin[:, B:], fin[:, :B])
    swap = remote(FSND, FIN.at[c], z_recv.at[5], dev_c)
    go(swap)

    def put_own(t, _):
        rows = pl.ds(pl.multiple_of(t * 256, 256), 256)
        P1[rows, :] = jnp.dot(
            XN[rows, pl.ds(pl.multiple_of(c * HALF, B), HALF)], FIN[c], preferred_element_type=F32
        ).astype(BF16)
        return 0

    lax.fori_loop(0, 8, put_own, 0)
    swap.wait_recv()
    cols = pl.ds(pl.multiple_of((2 * z + c) * B, B), B)

    def put(t, _):
        rows = pl.ds(pl.multiple_of(t * 256, 256), 256)
        part = jnp.dot(
            XN[rows, pl.ds(pl.multiple_of((1 - c) * HALF, B), HALF)], FIN[1 - c],
            preferred_element_type=F32,
        )
        value = part + P1[rows, :].astype(F32)
        old = X[rows, cols].astype(F32)
        OUT[rows, :] = jnp.where(LIVE[rows, :].astype(F32) > 0.5, value, old).astype(BF16)
        store(t).start()
        return 0

    def store(t):
        rows = pl.ds(pl.multiple_of(t * 256, 256), 256)
        return pltpu.make_async_copy(OUT.at[rows, :], out_ref.at[rows, :], lsem.at[5 + t])

    lax.fori_loop(0, 8, put, 0)
    for t in range(8):
        store(t).wait()
    drain(0)


def body(
    tokens, segment_ids, row_order, row_counts, first_gain, second_gain,
    query_weight, key_weight, value_weight, output_weight, gate_weight, up_weight, down_weight,
):
    vm = pl.BlockSpec(memory_space=pltpu.VMEM)
    anyspace = pl.BlockSpec(memory_space=pl.ANY)
    smem = pl.BlockSpec(memory_space=pltpu.SMEM)
    return pl.pallas_call(
        kernel,
        out_shape=jax.ShapeDtypeStruct((ROWS, B), BF16),
        in_specs=[anyspace] * 3 + [smem] + [anyspace] * 9,
        out_specs=anyspace,
        scratch_shapes=[
            pltpu.VMEM((NX, NY, 2, BLOCKS, B, B), BF16),
            pltpu.VMEM((ROWS, D), BF16),
            pltpu.VMEM((ROWS, D), BF16),
            pltpu.VMEM((ROWS, B), BF16),
            pltpu.VMEM((ROWS + 512, B), BF16),
            pltpu.VMEM((ROWS + 512, B), BF16),
            pltpu.VMEM((ROWS, B), BF16),
            pltpu.VMEM((2 * HALF, ROWS), BF16),
            pltpu.VMEM((2 * HALF, B), BF16),
            pltpu.VMEM((16, PIECE, B), BF16),
            pltpu.VMEM((NZ, PIECE, D), BF16),
            pltpu.VMEM((HALF, D), BF16),
            pltpu.VMEM((HALF, 1024), BF16),
            pltpu.VMEM((2, 4, 2, QTR, 2 * B), BF16),
            pltpu.VMEM((2, QTR, 2 * B), BF16),
            pltpu.VMEM((2, HALF, B), BF16),
            pltpu.VMEM((HALF, B), BF16),
            pltpu.VMEM((ROWS, B), BF16),
            pltpu.VMEM((ROWS, B), BF16),
            pltpu.VMEM((ROWS, B), BF16),
            pltpu.VMEM((24, B), F32),
            pltpu.VMEM((NBLK, B), F32),
            pltpu.VMEM((NBLK, B), F32),
            pltpu.VMEM((NBLK, B), jnp.int32),
            pltpu.VMEM((NBLK, B), jnp.int32),
            pltpu.VMEM((NBLK, B), F32),
            pltpu.VMEM((NBLK, B), F32),
            pltpu.SemaphoreType.DMA((17,)),
            pltpu.SemaphoreType.DMA((SENDS,)),
            pltpu.SemaphoreType.DMA((30,)),
            pltpu.SemaphoreType.DMA((34,)),
        ],
        compiler_params=pltpu.CompilerParams(
            collective_id=0, has_side_effects=True, vmem_limit_bytes=67 * 1000 * 1000
        ),
        name="recursion_step",
    )(
        tokens,
        segment_ids.reshape(NBLK, B),
        row_order.reshape(NBLK, B),
        row_counts,
        first_gain.reshape(NBLK, B),
        second_gain.reshape(NBLK, B),
        query_weight, key_weight, value_weight, output_weight,
        gate_weight, up_weight, down_weight,
    )


def solution(mesh):
    weight = P("fsdp", ("dp", "tensor"))
    weight_t = P(("dp", "tensor"), "fsdp")
    in_specs = (
        P("fsdp", None), P("fsdp"), P("fsdp"), P(), P(), P(),
        weight, weight, weight, weight_t, weight, weight, weight_t,
    )
    return jax.shard_map(
        body, mesh=mesh, in_specs=in_specs, out_specs=weight, check_vma=False
    )
```

```python
import math

import jax
import jax.numpy as jnp
from jax import lax
from jax.experimental import pallas as pl
from jax.experimental.pallas import tpu as pltpu
from jax.sharding import PartitionSpec as P

F32 = jnp.float32
BF16 = jnp.bfloat16
NZ = 8
NX = 4
NY = 4
B = 128
ROWS = 2048
D = 2048
HALF = 640
QTR = 320
NBLK = 16
PIECE = 80
O_AT, G_AT, U_AT, D_AT, BLOCKS = 3, 11, 15, 19, 23
SENDS = 96
SLOT = {0: 0, 1: 1, -1: 2, 2: 3, -2: 4, 3: 5, -3: 6, 4: 7, -4: 7}
STEP_OF_SLOT = (0, 1, 7, 2, 6, 3, 5, 4)


def column_of(row):
    return jnp.transpose(jnp.broadcast_to(row, (B, B)))


def kernel(
    tok_hbm, seg_hbm, ord_hbm, cnt_ref, g1_hbm, g2_hbm,
    wq, wk, wv, wo, wg, wu, wd,
    out_ref,
    W, X, XN, q, k, v, att, OHP, PICK, A2, AGB, NRM, H, RS2, RB2, FIN, FSND, P1, LIVE, OUT,
    segf, ordf, ordm, seg_ref, ord_ref, g1_ref, g2_ref,
    lsem, ssem, wrecv, z_recv,
):
    z = lax.axis_index("dp")
    j = lax.axis_index("fsdp")
    c = lax.axis_index("tensor")
    x = j // NY
    y = lax.rem(j, NY)
    xp = lax.rem(x + 1, NX)
    xm = lax.rem(x + 3, NX)
    x2 = lax.rem(x + 2, NX)
    yp = lax.rem(y + 1, NY)
    ym = lax.rem(y + 3, NY)
    y2 = lax.rem(y + 2, NY)
    dev_xp = {"fsdp": xp * NY + y}
    dev_xm = {"fsdp": xm * NY + y}
    dev_yp = {"fsdp": x * NY + yp}
    dev_ym = {"fsdp": x * NY + ym}
    dev_c = {"tensor": 1 - c}

    def z_at(step):
        return lax.rem(z + step, NZ)

    def dev_z(step, other=0):
        if other:
            return {"dp": z_at(step), "tensor": 1 - c}
        return {"dp": z_at(step)}

    barrier = pltpu.get_barrier_semaphore()
    peers = [dev_xp, dev_xm, dev_yp, dev_ym, dev_c]
    peers += [dev_z(dz, other) for dz in range(1, NZ) for other in (0, 1)]
    for dev in peers:
        pl.semaphore_signal(barrier, inc=1, device_id=dev, device_id_type=pl.DeviceIdType.MESH)

    own = W.at[x, y, c]
    spots = [(wq, 0), (wk, 1), (wv, 2), (wo, O_AT)]
    spots += [(wg.at[:, pl.ds(i * B, B)], G_AT + i) for i in range(4)]
    spots += [(wu.at[:, pl.ds(i * B, B)], U_AT + i) for i in range(4)]
    spots += [(wd.at[pl.ds(i * B, B), :], D_AT + i) for i in range(4)]
    of_local = [0] * 3 + [1] + [2] * 4 + [3] * 4 + [4] * 4
    local = [
        pltpu.make_async_copy(ref, own.at[b], lsem.at[of_local[i]])
        for i, (ref, b) in enumerate(spots)
    ]
    for i in range(4):
        local[i].start()
    tok = [
        pltpu.make_async_copy(
            tok_hbm.at[pl.ds(i * 256, 256), :], X.at[pl.ds(i * 256, 256), :], lsem.at[5 + i]
        )
        for i in range(8)
    ]
    small = [
        pltpu.make_async_copy(src, dst, lsem.at[13 + i])
        for i, (src, dst) in enumerate(
            ((seg_hbm, seg_ref), (ord_hbm, ord_ref), (g1_hbm, g1_ref), (g2_hbm, g2_ref))
        )
    ]
    for cp in small:
        cp.start()
    for i in range(8):
        tok[i].start()
    for i in range(4, 16):
        local[i].start()

    pl.semaphore_wait(barrier, len(peers))

    sent, free = [], list(range(SENDS))

    class Remote:
        def __init__(self, src, dst, rs, dev):
            self.parts = src, dst, rs, dev

        def make(self):
            src, dst, rs, dev = self.parts
            self.slot = free.pop(0)
            self.copy = pltpu.make_async_remote_copy(
                src_ref=src, dst_ref=dst, send_sem=ssem.at[self.slot], recv_sem=rs,
                device_id=dev, device_id_type=pl.DeviceIdType.MESH,
            )
            sent.append(self)

        def start(self):
            self.make()
            self.copy.start()

        def wait_recv(self):
            self.copy.wait_recv()

    remote = Remote

    def go(cp):
        cp.start()

    def go_on_even(cp):
        cp.make()

        @pl.when(c == 0)
        def _():
            cp.copy.start()

        return cp.copy

    def arrived(ref, rs):
        pltpu.make_async_copy(ref, ref, rs).wait()

    def drain(keep):
        while len(sent) > keep:
            cp = sent.pop(0)
            cp.copy.wait_send()
            free.append(cp.slot)

    used = []

    def recv_sem(g, s):
        if (g, s) not in used:
            used.append((g, s))
        return wrecv.at[used.index((g, s))]

    def plan(g, a, b, local_at=None, kind="whole"):
        nb = pl.ds(a, b - a)
        up, dn = pl.ds(0, 64), pl.ds(64, 64)
        full = pl.ds(0, 4)
        lo, hi = pl.ds(0, 2), pl.ds(2, 2)

        def cp(s, idx, dev):
            ref = W.at[idx]
            return remote(ref, ref, recv_sem(g, s), dev)

        sizes = ((0, lo, 0, nb), (0, 0, 0, nb), (lo, full, 0, nb), (0, full, 0, nb))

        copies = [
            ((x, y, c, nb, up), dev_xp),
            ((x, y, c, nb, up), dev_xm),
            ((x, y, c, nb, dn), dev_yp),
            ((x, y, c, nb, dn), dev_ym),
            ((xm, y, c, nb, pl.ds(0, 32)), dev_xp),
            ((xp, y, c, nb, pl.ds(32, 32)), dev_xm),
            ((x, ym, c, nb, pl.ds(64, 32)), dev_yp),
            ((x, yp, c, nb, pl.ds(96, 32)), dev_ym),
            ((full, y, c, nb, up), dev_yp),
            ((full, y, c, nb, up), dev_ym),
            ((x, full, c, nb, dn), dev_xp),
            ((x, full, c, nb, dn), dev_xm),
            ((lo, ym, c, nb, up), dev_yp),
            ((hi, yp, c, nb, up), dev_ym),
            ((xm, lo, c, nb, dn), dev_xp),
            ((xp, hi, c, nb, dn), dev_xm),
        ]
        pass_on = [
            ((x, y, c, nb),),
            ((xm, y, c, nb, up), (xp, y, c, nb, up), (x, ym, c, nb, dn), (x, yp, c, nb, dn)),
            ((x2, y, c, nb, up), (x, y2, c, nb, dn)),
            ((full, ym, c, nb, up), (full, yp, c, nb, up), (xm, full, c, nb, dn), (xp, full, c, nb, dn)),
            ((full, y2, c, nb, up), (x2, full, c, nb, dn)),
        ]
        if kind == "second":
            pass_on[2] = ((full, y, c, nb, up), (x, full, c, nb, dn))
        if kind in ("first", "alone"):
            pass_on = [()] * 5

        held = []

        def stage(s, core=None):
            if core == 1:
                @pl.when(c == 1)
                def _():
                    for h in held:
                        h.start()
                return
            if s == 5:
                arrived(W.at[full, full, 1 - c, nb], recv_sem(g, 4))
                return
            if s == 0:
                arrived(own.at[nb], lsem.at[local_at])
            elif not (kind == "second" and s == 2):
                arrived(W.at[sizes[s - 1]], recv_sem(g, s - 1))
            if s < 4 and not (kind == "first" and s == 2):
                for i in range(4 * s, 4 * s + 4):
                    if core == 0:
                        held.append(go_on_even(cp(s, *copies[i])))
                    else:
                        go(cp(s, *copies[i]))
            for idx in pass_on[s]:
                go(cp(4, idx, dev_c))

        return stage

    w_q = plan(0, 0, 3, 0, "alone")
    w_a = plan(1, O_AT, O_AT + 1, 1, "first")
    w_c0 = plan(2, O_AT, O_AT + 3, None, "second")
    w_c1 = plan(3, O_AT + 3, O_AT + 5, None, "second")
    w_c2 = plan(4, O_AT + 5, O_AT + 8, None, "second")
    w_g = plan(5, G_AT, U_AT, 2)
    w_u = plan(6, U_AT, D_AT, 3)
    w_d = plan(7, D_AT, BLOCKS, 4)

    def ring_o(s):
        if s > 0:
            arrived(W.at[pl.ds(0, 4), 0, 0, pl.ds(0, 2 if s < 4 else 1)], z_recv.at[s - 1])
        for part in (0, 1):
            for d in (0, 1):
                if s < 3 or (s == 3 and part == d):
                    sign = 1 if d else -1
                    here, there = O_AT + SLOT[sign * s], O_AT + SLOT[sign * (s + 1)]
                    if part == 0:
                        src = W.at[pl.ds(0, 4), y, c, here, pl.ds(0, 64)]
                        dst = W.at[pl.ds(0, 4), y, c, there, pl.ds(0, 64)]
                    else:
                        src = W.at[x, pl.ds(0, 4), c, here, pl.ds(64, 64)]
                        dst = W.at[x, pl.ds(0, 4), c, there, pl.ds(64, 64)]
                    go(remote(src, dst, z_recv.at[s], dev_z(7 if d else 1)))

    w_q(0)
    w_a(0)
    w_g(0)

    for cp in small:
        cp.wait()
    segf[pl.ds(0, 8), :] = jnp.full((8, B), -1.0, F32)
    segf[pl.ds(4, NBLK), :] = seg_ref[...].astype(F32)
    k[pl.ds(0, 512), :] = jnp.zeros((512, B), BF16)
    v[pl.ds(0, 512), :] = jnp.zeros((512, B), BF16)
    order = ord_ref[...].astype(F32)
    ordf[...] = order
    rank = lax.broadcasted_iota(jnp.int32, (NBLK, B), 0) * B + lax.broadcasted_iota(
        jnp.int32, (NBLK, B), 1
    )
    ordm[...] = jnp.where(rank < cnt_ref[j], order, -1.0)
    gain1 = jnp.concatenate([g1_ref[pl.ds(i, 1), :] for i in range(NBLK)], axis=1)
    gain2 = jnp.concatenate([g2_ref[pl.ds(i, 1), :] for i in range(NBLK)], axis=1)

    def normed(data, gain):
        f = data.astype(F32)
        inv = lax.rsqrt(jnp.mean(f * f, axis=-1, keepdims=True) + 1e-05)
        return (f * inv * gain).astype(BF16)

    def norm_chunk(i):
        tok[i].wait()

        def body(r, _):
            rows = pl.ds(pl.multiple_of(i * 256 + r * 16, 16), 16)
            XN[rows, :] = normed(X[rows, :], gain1)
            return 0

        lax.fori_loop(0, 16, body, 0, unroll=4)

    lane = lax.broadcasted_iota(jnp.int32, (B, B), 1).astype(F32)
    sub = lax.broadcasted_iota(jnp.int32, (B, B), 0).astype(F32)

    def one_hot(t, _):
        rows = pl.ds(pl.multiple_of(t * B, B), B)
        col = column_of(ordf[pl.ds(t, 1), :])
        for u in range(NBLK):
            OHP[rows, pl.ds(u * B, B)] = jnp.where(col == lane + (B * u), 1.0, 0.0).astype(BF16)
        return 0

    norm_chunk(0)
    norm_chunk(1)
    norm_chunk(2)
    w_q(1)
    w_a(1)
    w_u(0)
    norm_chunk(3)
    norm_chunk(4)
    w_q(2)
    w_a(2)
    ring_o(0)
    w_g(1)
    w_d(0)
    norm_chunk(5)
    norm_chunk(6)
    norm_chunk(7)
    lax.fori_loop(0, 10, one_hot, 0)
    ring_o(1)
    w_q(3)
    w_u(1)
    drain(24)
    ring_o(2)
    w_q(4)
    w_c0(2)
    w_d(1)
    w_c1(2)

    def blocks(cc, b, count):
        return jnp.concatenate(
            [
                jnp.concatenate([W[i // NY, i % NY, cc, b + e] for e in range(count)], axis=1)
                for i in range(16)
            ],
            axis=0,
        )

    def qkv_product(m):
        rows = pl.ds(pl.multiple_of(m * 256, 256), 256)
        return jnp.dot(XN[rows, :], blocks(c, 0, 3), preferred_element_type=F32).astype(BF16)

    def qkv_store(m, r):
        rows = pl.ds(pl.multiple_of(m * 256, 256), 256)
        q[rows, :] = r[:, 0:B]
        rows = pl.ds(pl.multiple_of(512 + m * 256, 256), 256)
        k[rows, :] = r[:, B : 2 * B]
        v[rows, :] = r[:, 2 * B : 3 * B]

    scale = math.log2(math.e) / math.sqrt(B)
    below = lax.broadcasted_iota(jnp.int32, (256, 256), 1) <= lax.broadcasted_iota(
        jnp.int32, (256, 256), 0
    )

    def scores(i):
        qrows = pl.ds(pl.multiple_of(i * 256, 256), 256)
        krows = pl.ds(pl.multiple_of(i * 256, 256), 768)
        return lax.dot_general(
            q[qrows, :], k[krows, :], (((1,), (1,)), ((), ())), preferred_element_type=F32
        )

    def attend(i, s):
        krows = pl.ds(pl.multiple_of(i * 256, 256), 768)
        segq = jnp.concatenate(
            [column_of(segf[pl.ds(2 * i + 4 + e, 1), :]) for e in range(2)], axis=0
        )
        parts = [
            jnp.where(segq == segf[pl.ds(2 * i + t, 1), :], s[:, t * B : (t + 1) * B], -1e30)
            for t in range(6)
        ]
        s = jnp.concatenate(
            parts[:4]
            + [jnp.where(below[:, e * B : (e + 1) * B], parts[4 + e], -1e30) for e in range(2)],
            axis=1,
        )
        e = jnp.exp2((s - jnp.max(s, axis=-1, keepdims=True)) * scale)
        p = (e * (1.0 / jnp.sum(e, axis=-1, keepdims=True))).astype(BF16)
        return jnp.dot(p, v[krows, :], preferred_element_type=F32).astype(BF16)

    def att_store(i, value):
        att[pl.ds(pl.multiple_of(i * 256, 256), 256), :] = value

    def both(m, _):
        raw = scores(m - 1)
        r = qkv_product(m)
        done = attend(m - 1, raw)
        att_store(m - 1, done)
        qkv_store(m, r)
        return 0

    qkv_store(0, qkv_product(0))
    lax.fori_loop(1, 4, both, 0)
    ring_o(3)
    lax.fori_loop(4, 7, both, 0)
    w_c0(3)
    ring_o(4)
    w_c2(2)
    w_c1(3)
    lax.fori_loop(7, 8, both, 0)
    att_store(7, attend(7, scores(7)))
    drain(32)

    def pick(cc):
        def tile(t, _):
            rows = pl.ds(pl.multiple_of(cc * HALF + t * QTR, 64), QTR)
            PICK[rows, :] = jnp.dot(
                OHP[rows, :], att[...], preferred_element_type=F32
            ).astype(BF16)
            return 0

        lax.fori_loop(0, 2, tile, 0)

    def piece_rows(zs, cc):
        return pl.ds(pl.multiple_of(cc * HALF + zs * PIECE, 16), PIECE)

    for other in (1, 0):
        cc = 1 - c if other else c
        pick(cc)
        for dz in (4, 3, 5, 2, 6, 1, 7, 0):
            if dz == 0 and other == 0:
                continue
            dev = dev_z(dz, other) if dz else dev_c
            go(remote(PICK.at[piece_rows(z_at(dz), cc)], A2.at[2 * z + c], z_recv.at[4], dev))
    A2[2 * z + c] = PICK[piece_rows(z, c), :]

    def row_tokens(n, _):
        cols = pl.ds(pl.multiple_of(n * 256, 256), 256)
        AGB[z, :, cols] = jnp.dot(
            OHP[piece_rows(z, c), :], X[:, cols], preferred_element_type=F32
        ).astype(BF16)
        return 0

    lax.fori_loop(0, 4, row_tokens, 0)
    w_c2(3)
    w_c0(4)
    w_c1(4)
    w_g(2, 0)
    w_u(2, 0)

    lax.fori_loop(4, 8, row_tokens, 0)
    w_c2(4)

    def put_hot(t, _):
        rows = pl.ds(pl.multiple_of(t * B, B), B)
        base = (t * B).astype(F32)
        for u in range(10):
            XN[rows, pl.ds(u * B, B)] = jnp.where(
                ordm[pl.ds(u, 1), :] == sub + base, 1.0, 0.0
            ).astype(BF16)
        return 0

    ones = jnp.ones((2 * HALF, B), BF16)

    def live(t, _):
        rows = pl.ds(pl.multiple_of(t * 256, 256), 256)
        LIVE[rows, :] = jnp.dot(
            XN[rows, pl.ds(0, 2 * HALF)], ones, preferred_element_type=F32
        ).astype(BF16)
        return 0

    arrived(A2.at[pl.ds(0, 15)], z_recv.at[4])
    w_g(2, 1)
    w_u(2, 1)
    w_c0(5)
    w_c1(5)
    w_c2(5)

    def w_index(n):
        return n // 2, 2 * lax.rem(n, 2)

    def ring_copy(base, src, dst, d, s, h):
        n = base + d * 7 + ((0 if s == 0 else 2 * s - 1 + h) if base == 20 else (6 if s == 3 else 2 * s + h))
        return remote(src, dst, z_recv.at[n], dev_z(1) if d == 0 else dev_z(7))

    ag = {}

    def ag_copy(d, s, h):
        if (d, s, h) not in ag:
            src = z_at(NZ - s) if d == 0 else z_at(s)
            ref = AGB.at[src, :, pl.ds(h * 1024, 1024)]
            ag[d, s, h] = ring_copy(6, ref, ref, d, s, h)
        return ag[d, s, h]

    def out_proj(n, _):
        xw, yw = w_index(n)
        cols = pl.ds(pl.multiple_of(n * 256, 256), 256)
        rhs = jnp.concatenate(
            [
                jnp.concatenate([W[xw, yw + e, cc, O_AT + slot] for e in range(2)], axis=1)
                for slot in range(8)
                for cc in range(2)
            ],
            axis=0,
        )
        lhs = jnp.concatenate(
            [A2[2 * z_at(STEP_OF_SLOT[slot]) + cc] for slot in range(8) for cc in range(2)], axis=1
        )
        total = jnp.dot(lhs, rhs, preferred_element_type=F32)
        AGB[z, :, cols] = (AGB[z, :, cols].astype(F32) + total).astype(BF16)
        return 0

    for h in (0, 1):
        lax.fori_loop(4 * h, 4 * h + 4, out_proj, 0)
        for d in (0, 1):
            go(ag_copy(d, 0, h))

    batches = ([z, z_at(1), z_at(7), z_at(2)], [z_at(6), z_at(3), z_at(5)], [z_at(4)])

    def prepare(at):
        zs = sum(batches, [])[at]
        for r in range(0, PIECE, 16):
            NRM[pl.ds(at * PIECE + r, 16), :] = normed(AGB[zs, pl.ds(r, 16), :], gain2)

    def ff_in(batch, begin=0, end=4):
        def body(n, _):
            cc = n // 2
            e = 2 * lax.rem(n, 2)
            lhs = NRM[pl.ds((0, 4, 7)[batch] * PIECE, len(batches[batch]) * PIECE), :]
            g = jnp.dot(lhs, blocks(cc, G_AT + e, 2), preferred_element_type=F32)
            u = jnp.dot(lhs, blocks(cc, U_AT + e, 2), preferred_element_type=F32)
            hid = (g / (1.0 + jnp.exp(-g)) * u).astype(BF16)
            cols = pl.ds(pl.multiple_of(n * 256, 256), 256)
            for i, zs in enumerate(batches[batch]):
                H[pl.ds(pl.multiple_of(zs * PIECE, 16), PIECE), cols] = hid[
                    i * PIECE : (i + 1) * PIECE
                ]
            return 0

        lax.fori_loop(begin, end, body, 0)

    def receive(s, h):
        for d in (0, 1):
            if s == 3 and h != d:
                continue
            ag_copy(d, s, h).wait_recv()
            if s < 2 or (s == 2 and h == d):
                go(ag_copy(d, s + 1, h))

    prepare(0)
    lax.fori_loop(0, 16, put_hot, 0)
    w_g(3)
    lax.fori_loop(0, 8, live, 0)
    receive(0, 0)
    drain(40)
    w_u(3)
    w_d(2)
    receive(0, 1)
    prepare(1)
    prepare(2)
    drain(40)
    receive(1, 0)
    w_g(4)
    receive(1, 1)
    prepare(3)
    prepare(4)
    w_u(4)
    receive(2, 0)
    w_g(5)
    w_u(5)
    ff_in(0, 0, 2)
    receive(2, 1)
    w_d(3)
    ff_in(0, 2, 4)
    drain(40)
    prepare(5)
    prepare(6)
    ff_in(1)
    w_d(4)
    receive(3, 0)
    receive(3, 1)
    prepare(7)
    ff_in(2)
    w_d(5)

    def rows_of(h):
        return pl.ds(h * QTR, QTR)

    def partial(zd, h):
        xw, yw = w_index(zd)
        rhs = jnp.concatenate(
            [
                jnp.concatenate([W[xw, yw + e, cc, D_AT + b] for e in range(2)], axis=1)
                for cc in range(2)
                for b in range(4)
            ],
            axis=0,
        )
        return jnp.dot(H[rows_of(h), :], rhs, preferred_element_type=F32)

    copies = {}
    for d in (0, 1):
        RB2[d] = partial(z_at(4), d).astype(BF16)
        copies[d, 0, d] = ring_copy(20, RB2.at[d], RS2.at[d, 0, d], d, 0, d)
        go(copies[d, 0, d])
    for s in (1, 2, 3):
        for d, h in ((0, 1), (1, 0), (0, 0), (1, 1)):
            part = partial(z_at(4 - s) if d == 0 else z_at(4 + s), h)
            slot = RS2.at[d, s - 1, h]
            if (d, s - 1, h) in copies:
                copies[d, s - 1, h].wait_recv()
                part = part + slot[...].astype(F32)
            slot[...] = part.astype(BF16)
            copies[d, s, h] = ring_copy(20, slot, RS2.at[d, s, h], d, s, h)
            go(copies[d, s, h])
        drain(16)
    mine = pl.ds(pl.multiple_of(z * 256, 256), 256)
    for h in (1, 0):
        total = partial(z, h)
        copies[0, 3, h].wait_recv()
        copies[1, 3, h].wait_recv()
        total = total + RS2[0, 3, h].astype(F32) + RS2[1, 3, h].astype(F32)
        carried = jnp.concatenate([AGB[4 * h + i, :, mine] for i in range(4)], axis=0)
        fin = (carried.astype(F32) + total).astype(BF16)
        FIN[c, rows_of(h), :] = jnp.where(c == 0, fin[:, :B], fin[:, B:])
        FSND[rows_of(h), :] = jnp.where(c == 0, fin[:, B:], fin[:, :B])
    swap = remote(FSND, FIN.at[c], z_recv.at[5], dev_c)
    go(swap)

    def put_own(t, _):
        rows = pl.ds(pl.multiple_of(t * 256, 256), 256)
        P1[rows, :] = jnp.dot(
            XN[rows, pl.ds(pl.multiple_of(c * HALF, B), HALF)], FIN[c], preferred_element_type=F32
        ).astype(BF16)
        return 0

    lax.fori_loop(0, 8, put_own, 0)
    swap.wait_recv()
    cols = pl.ds(pl.multiple_of((2 * z + c) * B, B), B)

    def put(t, _):
        rows = pl.ds(pl.multiple_of(t * 256, 256), 256)
        part = jnp.dot(
            XN[rows, pl.ds(pl.multiple_of((1 - c) * HALF, B), HALF)], FIN[1 - c],
            preferred_element_type=F32,
        )
        value = part + P1[rows, :].astype(F32)
        old = X[rows, cols].astype(F32)
        OUT[rows, :] = jnp.where(LIVE[rows, :].astype(F32) > 0.5, value, old).astype(BF16)
        store(t).start()
        return 0

    def store(t):
        rows = pl.ds(pl.multiple_of(t * 256, 256), 256)
        return pltpu.make_async_copy(OUT.at[rows, :], out_ref.at[rows, :], lsem.at[5 + t])

    lax.fori_loop(0, 8, put, 0)
    for t in range(8):
        store(t).wait()
    drain(0)


def body(
    tokens, segment_ids, row_order, row_counts, first_gain, second_gain,
    query_weight, key_weight, value_weight, output_weight, gate_weight, up_weight, down_weight,
):
    vm = pl.BlockSpec(memory_space=pltpu.VMEM)
    anyspace = pl.BlockSpec(memory_space=pl.ANY)
    smem = pl.BlockSpec(memory_space=pltpu.SMEM)
    return pl.pallas_call(
        kernel,
        out_shape=jax.ShapeDtypeStruct((ROWS, B), BF16),
        in_specs=[anyspace] * 3 + [smem] + [anyspace] * 9,
        out_specs=anyspace,
        scratch_shapes=[
            pltpu.VMEM((NX, NY, 2, BLOCKS, B, B), BF16),
            pltpu.VMEM((ROWS, D), BF16),
            pltpu.VMEM((ROWS, D), BF16),
            pltpu.VMEM((ROWS, B), BF16),
            pltpu.VMEM((ROWS + 512, B), BF16),
            pltpu.VMEM((ROWS + 512, B), BF16),
            pltpu.VMEM((ROWS, B), BF16),
            pltpu.VMEM((2 * HALF, ROWS), BF16),
            pltpu.VMEM((2 * HALF, B), BF16),
            pltpu.VMEM((16, PIECE, B), BF16),
            pltpu.VMEM((NZ, PIECE, D), BF16),
            pltpu.VMEM((HALF, D), BF16),
            pltpu.VMEM((HALF, 1024), BF16),
            pltpu.VMEM((2, 4, 2, QTR, 2 * B), BF16),
            pltpu.VMEM((2, QTR, 2 * B), BF16),
            pltpu.VMEM((2, HALF, B), BF16),
            pltpu.VMEM((HALF, B), BF16),
            pltpu.VMEM((ROWS, B), BF16),
            pltpu.VMEM((ROWS, B), BF16),
            pltpu.VMEM((ROWS, B), BF16),
            pltpu.VMEM((24, B), F32),
            pltpu.VMEM((NBLK, B), F32),
            pltpu.VMEM((NBLK, B), F32),
            pltpu.VMEM((NBLK, B), jnp.int32),
            pltpu.VMEM((NBLK, B), jnp.int32),
            pltpu.VMEM((NBLK, B), F32),
            pltpu.VMEM((NBLK, B), F32),
            pltpu.SemaphoreType.DMA((17,)),
            pltpu.SemaphoreType.DMA((SENDS,)),
            pltpu.SemaphoreType.DMA((30,)),
            pltpu.SemaphoreType.DMA((34,)),
        ],
        compiler_params=pltpu.CompilerParams(
            collective_id=0, has_side_effects=True, vmem_limit_bytes=67 * 1000 * 1000
        ),
        name="recursion_step",
    )(
        tokens,
        segment_ids.reshape(NBLK, B),
        row_order.reshape(NBLK, B),
        row_counts,
        first_gain.reshape(NBLK, B),
        second_gain.reshape(NBLK, B),
        query_weight, key_weight, value_weight, output_weight,
        gate_weight, up_weight, down_weight,
    )


def solution(mesh):
    weight = P("fsdp", ("dp", "tensor"))
    weight_t = P(("dp", "tensor"), "fsdp")
    in_specs = (
        P("fsdp", None), P("fsdp"), P("fsdp"), P(), P(), P(),
        weight, weight, weight, weight_t, weight, weight, weight_t,
    )
    return jax.shard_map(
        body, mesh=mesh, in_specs=in_specs, out_specs=weight, check_vma=False
    )
```
